256 devices in a mesh: grp: 32 (over z_hi, x, core), fsdp: 8 (over z_lo, y).
Axes of the slice: x: 4, y: 4, z: 8 (z_hi: 4, z_lo: 2; z = z_hi * 2 + z_lo), core: 2. Of those that a mesh axis runs over, the one named last changes fastest.
Arguments:
- tokens: bfloat16 [98304, 3584], P(('grp', 'fsdp')), may hold values from -6 to 6
- target: bfloat16 [98304, 1024], P(('grp', 'fsdp')), may hold values from -6 to 6
- weight: bfloat16 [3584, 1024], P('fsdp'), may hold values from -0.09375 to 0.09375
- factor_a: bfloat16 [3584, 512], P('fsdp'), may hold values from -6 to 6
- factor_b: bfloat16 [512, 1024], replicated, may hold values from -6 to 6
- counts: int32 [512], replicated, may hold values from 1 to 768, 98304 in all
- cand_index: int32 [512, 2], replicated, may hold values from 0 to 511
Outputs:
- update: float32 [3584, 1024], P('fsdp')
- scores: float32 [512], replicated
The draws below stay inside these ranges and needn't reach their ends.
Inputs may be any that keep to these rules, and one draw needn't show every extreme that they name: The counts sum to 98304; candidate i owns the tokens from counts[0] + ... + counts[i-1] on.
All inputs are finite; a program needn't handle non-finite values.
Results may differ from the reference program's by a relative error of at most 0.003.
Values may be sent and summed in bfloat16 or wider, within the bound.
A program may use at most 64 MiB of HBM per device.

```python
import math
import jax
import jax.numpy as jnp
import numpy as np
from jax import lax

D = 3584
OUT = 1024
POOL = 512
TOK_DEV = 384
CANDS = 512
TOKENS = 98304


def plant(result, rng, smallest, top_value):
    place = [jax.random.randint(jax.random.fold_in(rng, axis), (), 0, length) for axis, length in enumerate(result.shape)]
    widest = result.shape.index(max(result.shape))
    beside = place[:widest] + [(place[widest] + 1) % result.shape[widest]] + place[widest + 1:]
    return result.at[tuple(place)].set(smallest).at[tuple(beside)].set(top_value)


def levels(own_key, shape, pieces, least, largest):
    def one(dim, blocks):
        steps = jax.random.uniform(jax.random.fold_in(jax.random.fold_in(own_key, 6), dim), (blocks,), jnp.float32, least / len(pieces), largest / len(pieces))
        return jnp.repeat(jnp.exp(steps), shape[dim] // blocks).reshape((-1,) + (1,) * (len(shape) - dim - 1))

    level = one(*pieces[0])
    for cut in pieces[1:]:
        level = level * one(*cut)
    return level


def length_profile(amount, total, reach, slope):
    portions = [(1 << 20) // math.isqrt(standing ** slope) + 1 for standing in range(2, amount + 1)]
    rest, holding = total - reach - (amount - 1), [1] * (amount - 1)
    while rest > 0:
        movable = [i for i in range(amount - 1) if holding[i] < reach]
        whole, remaining = sum([portions[i] for i in movable]), rest
        for i in movable:
            extra = min(reach - holding[i], max(1, remaining * portions[i] // whole), rest)
            holding[i] = holding[i] + extra
            rest = rest - extra
    return np.array([reach] + holding)


def ragged(stream_key, count, total, reach, skew):
    if count == 2:
        one = jax.random.randint(stream_key, (), max(1, total - reach), min(reach, total - 1) + 1)
        return jnp.stack([one, total - one])
    lengths = jnp.asarray(length_profile(count, total, reach, skew), jnp.int32)
    twos = (count - 1) // 2
    giver, receiver = lengths[1:1 + 2 * twos:2], lengths[2:2 + 2 * twos:2]
    room = jnp.minimum(giver - 1, reach - receiver)
    passed = jax.random.randint(jax.random.fold_in(stream_key, 1), (twos,), 0, 1 << 20) % (room + 1)
    lengths = lengths.at[1:1 + 2 * twos:2].set(giver - passed).at[2:2 + 2 * twos:2].set(receiver + passed)
    return lengths[jax.random.permutation(jax.random.fold_in(stream_key, 2), count)]


def bell_draw(own_key, dims, deviation, most, split=(), kind=jnp.bfloat16):
    factor_of = levels(own_key, dims, split, -0.22, 0.18) if split else 1.0
    values = jax.random.normal(own_key, dims, jnp.float32) * deviation * factor_of
    return jnp.minimum(jnp.maximum(values, -most), most).astype(kind)


def setup_inputs(seed: int = 0) -> dict:
    splits = jax.random.split(jax.random.key(seed), 8)
    tokens = bell_draw(splits[0], (TOKENS, D), 1.0, 6.0, ((0, 256),))
    target = bell_draw(splits[1], (TOKENS, OUT), 1.0, 6.0, ((0, 256),))
    weight = bell_draw(splits[2], (D, OUT), D ** -0.5, 0.09375, ((0, 8),))
    factor_a = bell_draw(splits[3], (D, POOL), 1.0, 6.0, ((0, 8),))
    factor_b = bell_draw(splits[4], (POOL, OUT), 1.0, 6.0)
    counts = ragged(splits[5], CANDS, TOKENS, 4 * TOKENS // CANDS, 2).astype(jnp.int32)
    cand_index = plant(jax.random.randint(splits[6], (CANDS, 2), 0, POOL), jax.random.fold_in(splits[6], 1), 0, POOL - 1).astype(jnp.int32)
    return {"tokens": tokens, "target": target, "weight": weight, "factor_a": factor_a, "factor_b": factor_b, "counts": counts, "cand_index": cand_index}


def reference(tokens, target, weight, factor_a, factor_b, counts, cand_index):
    noise = 0.5 * D ** (-0.5)
    ends = jnp.cumsum(counts).astype(jnp.int32)
    position = jnp.arange(TOKENS, dtype=jnp.int32)
    owner = jnp.searchsorted(ends, position, side='right').astype(jnp.int32)
    left_index = cand_index[:, 0]
    right_index = cand_index[:, 1]
    tok_a = jnp.take(left_index, owner)
    tok_b = jnp.take(right_index, owner)
    weight_wide = weight.astype(jnp.float32)
    pool_rows = factor_a.T.astype(jnp.float32)
    pool_right = factor_b.astype(jnp.float32)
    blocks = TOKENS // TOK_DEV

    def one_block(items):
        x_rows, t_rows, a_sel, b_sel = items
        x_wide = x_rows.astype(jnp.float32)
        base = jnp.dot(x_wide, weight_wide, precision=lax.Precision.HIGHEST)
        a_rows = jnp.take(pool_rows, a_sel, axis=0)
        score = lax.optimization_barrier(jnp.sum(x_wide * a_rows, axis=1))
        b_rows = jnp.take(pool_right, b_sel, axis=0)
        output = base + noise * score[:, None] * b_rows
        diff = output - t_rows.astype(jnp.float32)
        return lax.optimization_barrier(jnp.mean(diff * diff, axis=1))
    loss = lax.map(one_block, (tokens.reshape(blocks, TOK_DEV, D), target.reshape(blocks, TOK_DEV, OUT), tok_a.reshape(blocks, TOK_DEV), tok_b.reshape(blocks, TOK_DEV))).reshape(TOKENS)
    totals = jax.ops.segment_sum(loss, owner, num_segments=CANDS)
    fitness = -totals / counts.astype(jnp.float32)
    middle = jnp.mean(fitness)
    spread = jnp.mean((fitness - middle) ** 2)
    scores = (fitness - middle) / jnp.sqrt(spread + 1e-06)
    columns = jnp.take(factor_a, left_index, axis=1).astype(jnp.float32)
    scaled = (columns * scores[None, :]).astype(jnp.bfloat16)
    right_rows = jnp.take(factor_b, right_index, axis=0).astype(jnp.float32)
    update = jnp.dot(scaled.astype(jnp.float32), right_rows, precision=lax.Precision.HIGHEST) / jnp.sqrt(jnp.float32(CANDS))
    return (update, scores)
```

```python
import functools

import jax
import jax.numpy as jnp
from jax import lax
from jax.experimental import pallas as pl
from jax.experimental.pallas import tpu as pltpu
from jax.sharding import Mesh
from jax.sharding import PartitionSpec as P

D = 3584
F32 = jnp.float32
BF16 = jnp.bfloat16
MESH = pl.DeviceIdType.MESH
FSDP = ("fsdp_0", "fsdp_1")
GRP_FSDP = ("grp_0", "grp_1", "grp_2", "fsdp_0", "fsdp_1")

INBOUND = {
    "y+": ((0, 1, "m1"), (0, 1, "m2"), (0, 2, "m1"), (0, 1, "c2"), (0, 1, "c1"), (0, 2, "m2"), (0, 2, "c1"), (1, 2, "t2")),
    "y-": ((0, 3, "m1"), (0, 3, "m2"), (0, 3, "c1"), (0, 3, "c2"), (1, 3, "m2"), (0, 2, "c2"), (1, 2, "m2"), (1, 2, "c1")),
    "z+": ((1, 0, "m1"), (1, 0, "t1"), (1, 3, "m1"), (1, 1, "m1"), (1, 1, "t1"), (1, 3, "c1"), (1, 1, "c2"), (1, 2, "c2")),
    "z-": ((1, 0, "m2"), (1, 0, "c1"), (1, 0, "c2"), (1, 1, "m2"), (1, 2, "m1"), (1, 3, "c2"), (1, 1, "c1")),
    "x+": ((0, 1, "t1"), (1, 0, "t2"), (1, 3, "t1"), (0, 3, "t2"), (1, 3, "t2"), (0, 2, "t2")),
    "x-": ((0, 3, "t1"), (0, 1, "t2"), (0, 2, "t1"), (1, 1, "t2"), (1, 2, "t1")),
}
LINK_STEP = {"y+": (0, 1, 0), "y-": (0, -1, 0), "z+": (0, 0, 1), "z-": (0, 0, -1), "x+": (1, 0, 0), "x-": (-1, 0, 0)}
SWAP = {"m1": "t1", "m2": "t2", "t1": "m1", "t2": "m2"}
ROLES = ("m1", "m2", "t1", "t2", "c1", "c2")
GROUPS = {"a": ("m1", "t1"), "p": ("m2", "t2"), "q": ("c1", "c2")}
PIECE_US, HOP_US, LEAD_US, TOKENS_US = 2.48, 1.7, 2.5, 5.0


def source(link, o, d, role):
    if link == "y+":
        return (o, (d - 1) % 4, role)
    if link == "y-":
        return (o, (d + 1) % 4, role)
    if link[0] == "z":
        return (1 - o, d, role)
    return (o, d, SWAP[role])


def timeline():
    arrival = {(0, 0, role): 0.0 for role in ROLES}
    free = dict.fromkeys(INBOUND, 0.0)
    waiting = {link: list(items) for link, items in INBOUND.items()}
    events = []
    while any(waiting.values()):
        ready = [
            (max(free[link], arrival[source(link, *items[0])]), link)
            for link, items in waiting.items()
            if items and source(link, *items[0]) in arrival
        ]
        start, link = min(ready)
        item = waiting[link].pop(0)
        free[link] = start + PIECE_US
        arrival[item] = start + PIECE_US + HOP_US
        issue = max(arrival[source(link, *item)], start - LEAD_US)
        events.append((issue, 0, ("send", link, item)))
    for o in range(2):
        for d in range(4):
            for group, roles in GROUPS.items():
                when = max(TOKENS_US, *(arrival[(o, d, role)] for role in roles))
                events.append((when, 1, ("product", (o, d), group)))
    return events


def one_hot(row, first, size):
    lines = lax.broadcasted_iota(jnp.int32, (size, row.shape[1]), 0) + first
    return (lines == row).astype(F32).astype(BF16)


def across(a, b):
    return lax.dot_general(a, b, (((1,), (1,)), ((), ())), preferred_element_type=F32)


def kernel(
    tokens, target, weight, factor_a, factor_b, counts, index, totals, asel_out, bsel_out,
    tok, tgt, buf, fb, fa, cnt, idx, acc_a, acc_w, owns, picks, brow, s_part, s_recv, asel, bsel,
    ar_x, ar_y, ar_z, local, send_sem, recv_sem, tok_send, tok_recv, s_send, s_got, ar_send, ar_recv,
):
    zh, x, c, zl, y = (lax.axis_index(n) for n in GRP_FSDP)
    z = zh * 2 + zl
    par = lax.rem(x, 2)
    rows, depth, cands = tokens.shape[0], weight.shape[0], counts.shape[1]
    noise = 0.5 * D ** (-0.5)

    def at(dx=0, dy=0, dz=0, dc=0):
        there = lax.rem(z + dz + 8, 8)
        return (there // 2, lax.rem(x + dx + 4, 4), lax.rem(c + dc + 2, 2), lax.rem(there, 2), lax.rem(y + dy + 4, 4))

    def piece_of(role):
        return {"m1": par, "m2": 2 + par, "t1": 1 - par, "t2": 3 - par, "c1": 4, "c2": 5}[role]

    def rows_of(d):
        return pl.ds(pl.multiple_of(lax.rem(y + d, 2) * 64, 64), depth)

    def columns(start, size):
        return pl.ds(pl.multiple_of(start, 128), size)

    copies = {}

    def bring(name, src, dst):
        copies[name] = pltpu.make_async_copy(src, dst, local.at[len(copies)])
        copies[name].start()

    for role in ROLES:
        j = piece_of(role)
        if role in ("m1", "t1"):
            src = factor_a.at[:, columns(c * 256 + j * 128, 128)]
        else:
            src = weight.at[:, columns(c * 512 + (j - 2) * 128, 128)]
        bring(role, src, buf.at[0, j, rows_of(0)])
    bring("cnt", counts, cnt)
    bring("idx", index, idx)
    bring("tok", tokens, tok.at[0])
    bring("tgt", target.at[:, columns(c * 512, 512)], tgt.at[0])
    bring("fb", factor_b, fb)
    bring("fa", factor_a, fa)

    zero = jnp.zeros((64, 128), BF16)
    for d in range(4):
        gap = pl.multiple_of((1 - lax.rem(y + d, 2)) * depth, 64)
        for o in range(2):
            for j in range(6):
                buf[o * 4 + d, j, pl.ds(gap, 64), :] = zero

    ar_peers = [
        [dict(dx=dx, dc=dc) for dx in range(4) for dc in range(2) if dx or dc],
        [dict(dy=dy) for dy in range(1, 4)],
        [dict(dz=dz) for dz in range(1, 8)],
    ]
    barrier = pltpu.get_barrier_semaphore()
    for group in ar_peers:
        for peer in group:
            pl.semaphore_signal(barrier, inc=1, device_id=at(**peer), device_id_type=MESH)
    pl.semaphore_wait(barrier, sum(map(len, ar_peers)))

    items = [item for link in INBOUND for item in INBOUND[link]]
    sends, waited = [], set()

    def need(item):
        if item in waited:
            return
        waited.add(item)
        o, d, role = item
        if (o, d) == (0, 0):
            copies[role].wait()
            return
        k = items.index(item)
        place = buf.at[o * 4 + d, piece_of(role), rows_of(d)]
        pltpu.make_async_remote_copy(
            src_ref=place, dst_ref=place, send_sem=send_sem.at[k], recv_sem=recv_sem.at[k],
            device_id=at(dc=1), device_id_type=MESH,
        ).wait_recv()

    def send(link, item):
        so, sd, srole = source(link, *item)
        need((so, sd, srole))
        k = items.index(item)
        dx, dy, dz = LINK_STEP[link]
        j = piece_of(srole)
        copy = pltpu.make_async_remote_copy(
            src_ref=buf.at[so * 4 + sd, j, rows_of(sd)],
            dst_ref=buf.at[item[0] * 4 + item[1], j, rows_of(sd)],
            send_sem=send_sem.at[k], recv_sem=recv_sem.at[k],
            device_id=at(-dx, -dy, -dz), device_id_type=MESH,
        )
        copy.start()
        sends.append(copy)

    swaps = [
        pltpu.make_async_remote_copy(
            src_ref=src, dst_ref=dst, send_sem=tok_send.at[k], recv_sem=tok_recv.at[k],
            device_id=at(dc=1), device_id_type=MESH,
        )
        for k, (src, dst) in enumerate(
            ((tokens, tok.at[1]), (target.at[:, columns((1 - c) * 512, 512)], tgt.at[1]))
        )
    ]

    def start_swaps():
        for copy in swaps:
            copy.start()

    def owners():
        copies["cnt"].wait()
        copies["idx"].wait()
        count = cnt[...]
        upto = (
            lax.broadcasted_iota(jnp.int32, (cands, cands), 0) <= lax.broadcasted_iota(jnp.int32, (cands, cands), 1)
        ).astype(F32).astype(BF16)
        high = jnp.broadcast_to((count >> 7).astype(F32), (16, cands)).astype(BF16)
        low = jnp.broadcast_to((count & 127).astype(F32), (16, cands)).astype(BF16)
        ends = jnp.dot(high, upto, preferred_element_type=F32) * 128.0 + jnp.dot(
            low, upto, preferred_element_type=F32
        )
        ends = ends[0:1, :].astype(jnp.int32)
        starts = ends - count
        for i in range(2):
            who = lax.rem(c + i, 2)
            block = ((zh * 4 + x) * 2 + who) * 8 + zl * 4 + y
            token = lax.broadcasted_iota(jnp.int32, (rows, cands), 0) + block * rows
            owns[i] = ((starts <= token) & (token < ends)).astype(F32).astype(BF16)

    def left_picks():
        left = one_hot(idx[0:1, :], c * 256, 256)
        for i in range(2):
            picks[i] = across(owns[i], left)

    def right_rows():
        copies["fb"].wait()
        right = one_hot(idx[1:2, :], 0, fb.shape[0])
        mine = fb[:, columns(c * 512, 512)]
        for i in range(2):
            chosen = across(owns[i], right).astype(BF16)
            brow[i] = jnp.dot(chosen, mine, preferred_element_type=F32)

    out_copies = []

    def chosen_left():
        copies["fa"].wait()
        left = one_hot(idx[0:1, :], 0, fa.shape[1])
        asel[...] = jnp.dot(fa[...], left, preferred_element_type=F32).astype(BF16)
        copy = pltpu.make_async_copy(asel, asel_out, local.at[len(copies)])
        copy.start()
        out_copies.append(copy)

    def chosen_right():
        size = (cands, cands)
        line, lane = lax.broadcasted_iota(jnp.int32, size, 0), lax.broadcasted_iota(jnp.int32, size, 1)
        row = idx[1:2, :].astype(F32)
        column = jnp.sum(jnp.where(line == lane, row, 0.0), axis=1, keepdims=True)
        right = (column == lane.astype(F32)).astype(F32).astype(BF16)
        bsel[...] = jnp.dot(right, fb[...], preferred_element_type=F32).astype(BF16)
        copy = pltpu.make_async_copy(bsel, bsel_out, local.at[len(copies) + 1])
        copy.start()
        out_copies.append(copy)

    seen, left_over = set(), {"a": 8}
    s_copies = [
        pltpu.make_async_remote_copy(
            src_ref=s_part.at[i], dst_ref=s_recv.at[1 - i], send_sem=s_send.at[i], recv_sem=s_got.at[i],
            device_id=at(dc=1), device_id_type=MESH,
        )
        for i in range(2)
    ]

    def product(slot, group):
        o, d = slot
        for role in GROUPS[group]:
            need((o, d, role))
        first = lax.rem(zl + o, 2) * 4 + lax.rem(y + d, 4)
        window = columns(first // 2 * 896 + lax.rem(first, 2) * 384, 512)
        j = "apq".index(group) * 2
        block = jnp.concatenate([buf[o * 4 + d, j], buf[o * 4 + d, j + 1]], axis=1)
        acc, lanes = (acc_a, slice(0, 256)) if group == "a" else (acc_w, slice(j * 128 - 256, j * 128))
        for i in range(2):
            if i == 0 and "tok" not in waited:
                copies["tok"].wait()
            if i == 1 and "tok" not in waited:
                swaps[0].wait_recv()
                waited.add("tok")
            part = jnp.dot(tok[i, :, window], block, preferred_element_type=F32)
            if group in seen:
                acc[i, :, lanes] += part
            else:
                acc[i, :, lanes] = part
        seen.add(group)
        if group == "a":
            left_over["a"] -= 1
            if left_over["a"] == 0:
                for i in range(2):
                    kept = jnp.where(picks[i] > 0.5, acc_a[i], 0.0)
                    s_part[i] = kept[:, :128] + kept[:, 128:]
                    s_copies[i].start()

    def perturb():
        copies["tgt"].wait()
        swaps[1].wait_recv()
        for copy in s_copies:
            copy.wait_recv()
        for i in range(2):
            score = jnp.sum(s_part[i] + s_recv[i], axis=1, keepdims=True) * noise
            acc_w[i] += score * brow[i] - tgt[i].astype(F32)

    events = timeline()
    after_a = max(when for when, _, what in events if what[0] == "product" and what[2] == "a")
    events += [
        (0.05, 2, (start_swaps,)), (0.5, 2, (owners,)), (1.0, 2, (left_picks,)), (1.5, 2, (right_rows,)),
        (2.0, 2, (chosen_left,)), (2.5, 2, (chosen_right,)), (after_a + 1.2, 2, (perturb,)),
    ]
    for _, _, what in sorted(events, key=lambda event: event[:2]):
        if what[0] == "send":
            send(*what[1:])
        elif what[0] == "product":
            product(*what[1:])
        else:
            what[0]()

    total = jnp.zeros((1, cands), F32)
    for i in range(2):
        diff = acc_w[i]
        square = diff * diff
        square = (square[:, :128] + square[:, 128:256]) + (square[:, 256:384] + square[:, 384:])
        loss = jnp.sum(square, axis=1, keepdims=True) * (1.0 / 1024)
        total += jnp.sum(owns[i].astype(F32) * loss, axis=0, keepdims=True)
    first = 0
    for group, ring, me, number in (
        (ar_peers[0], ar_x, x * 2 + c, lambda dx=0, dc=0: lax.rem(x - dx + 4, 4) * 2 + lax.rem(c - dc + 2, 2)),
        (ar_peers[1], ar_y, y, lambda dy: lax.rem(y - dy + 4, 4)),
        (ar_peers[2], ar_z, z, lambda dz: lax.rem(z - dz + 8, 8)),
    ):
        ring[me] = total
        out = [
            pltpu.make_async_remote_copy(
                src_ref=ring.at[me], dst_ref=ring.at[me], send_sem=ar_send.at[first + k], recv_sem=ar_recv.at[first + k],
                device_id=at(**peer), device_id_type=MESH,
            )
            for k, peer in enumerate(group)
        ]
        for copy in out:
            copy.start()
        for k, peer in enumerate(group):
            place = ring.at[number(**peer)]
            pltpu.make_async_remote_copy(
                src_ref=place, dst_ref=place, send_sem=ar_send.at[first + k], recv_sem=ar_recv.at[first + k],
                device_id=at(**peer), device_id_type=MESH,
            ).wait_recv()
        total = ring[0]
        for k in range(1, ring.shape[0]):
            total += ring[k]
        sends.extend(out)
        first += len(group)
    totals[...] = total
    for copy in sends + swaps + s_copies:
        copy.wait_send()
    for copy in out_copies:
        copy.wait()


def gather_and_sum(tokens, target, weight, factor_a, factor_b, counts, index):
    rows, depth = tokens.shape[0], weight.shape[0]
    cands, pool, out = counts.shape[1], factor_a.shape[1], weight.shape[1]
    links = sum(map(len, INBOUND.values()))
    dma = pltpu.SemaphoreType.DMA
    return pl.pallas_call(
        kernel,
        name="gather_and_sum",
        out_shape=(
            jax.ShapeDtypeStruct((1, cands), F32),
            jax.ShapeDtypeStruct((depth, cands), BF16),
            jax.ShapeDtypeStruct((cands, out), BF16),
        ),
        in_specs=[pl.BlockSpec(memory_space=pl.ANY)] * 7,
        out_specs=(
            pl.BlockSpec(memory_space=pltpu.VMEM),
            pl.BlockSpec(memory_space=pl.ANY),
            pl.BlockSpec(memory_space=pl.ANY),
        ),
        scratch_shapes=[
            pltpu.VMEM((2, rows, D), BF16),
            pltpu.VMEM((2, rows, out // 2), BF16),
            pltpu.VMEM((8, 6, depth + 64, 128), BF16),
            pltpu.VMEM((pool, out), BF16),
            pltpu.VMEM((depth, pool), BF16),
            pltpu.VMEM((1, cands), jnp.int32),
            pltpu.VMEM((2, cands), jnp.int32),
            pltpu.VMEM((2, rows, pool // 2), F32),
            pltpu.VMEM((2, rows, out // 2), F32),
            pltpu.VMEM((2, rows, cands), BF16),
            pltpu.VMEM((2, rows, pool // 2), F32),
            pltpu.VMEM((2, rows, out // 2), F32),
            pltpu.VMEM((2, rows, 128), F32),
            pltpu.VMEM((2, rows, 128), F32),
            pltpu.VMEM((depth, cands), BF16),
            pltpu.VMEM((cands, out), BF16),
            pltpu.VMEM((8, 1, cands), F32),
            pltpu.VMEM((4, 1, cands), F32),
            pltpu.VMEM((8, 1, cands), F32),
            dma((14,)),
            dma((links,)),
            dma((links,)),
            dma((2,)),
            dma((2,)),
            dma((2,)),
            dma((2,)),
            dma((17,)),
            dma((17,)),
        ],
        compiler_params=pltpu.CompilerParams(collective_id=0, has_side_effects=True, vmem_limit_bytes=48 << 20),
    )(tokens, target, weight, factor_a, factor_b, counts, index)


def finish_kernel(totals, counts, asel, bsel, update, scores):
    cands = counts.shape[1]
    fitness = -totals[...] / counts[...].astype(F32)
    middle = jnp.mean(fitness, axis=1, keepdims=True)
    spread = jnp.mean((fitness - middle) ** 2, axis=1, keepdims=True)
    score = (fitness - middle) / jnp.sqrt(spread + 1e-06)
    scores[...] = score
    scaled = (asel[...].astype(F32) * score).astype(BF16)
    update[...] = jnp.dot(scaled, bsel[...], preferred_element_type=F32) * (cands**-0.5)


def finish(totals, counts, asel, bsel):
    depth, cands = asel.shape
    out = bsel.shape[1]
    block = depth // 4
    row = pl.BlockSpec((1, cands), lambda i: (0, 0))
    return pl.pallas_call(
        finish_kernel,
        name="finish",
        grid=(4,),
        out_shape=(jax.ShapeDtypeStruct((depth, out), F32), jax.ShapeDtypeStruct((1, cands), F32)),
        in_specs=[
            row,
            row,
            pl.BlockSpec((block, cands), lambda i: (i, 0)),
            pl.BlockSpec((cands, out), lambda i: (0, 0)),
        ],
        out_specs=(pl.BlockSpec((block, out), lambda i: (i, 0)), row),
    )(totals, counts, asel, bsel)


def per_device(tokens, target, weight, factor_a, factor_b, counts, cand_index):
    counts = counts.reshape(1, -1)
    totals, asel, bsel = gather_and_sum(tokens, target, weight, factor_a, factor_b, counts, cand_index.T)
    update, scores = finish(totals, counts, asel, bsel)
    return (update, scores.reshape(-1))


def solution(mesh):
    split = Mesh(mesh.devices.reshape(4, 4, 2, 2, 4), GRP_FSDP)
    placed = (P(GRP_FSDP, None), P(GRP_FSDP, None), P(FSDP, None), P(FSDP, None), P(), P(), P())
    return jax.shard_map(
        per_device, mesh=split, in_specs=placed, out_specs=(P(FSDP, None), P()), check_vma=False
    )
```

```python
import functools

import jax
import jax.numpy as jnp
from jax import lax
from jax.experimental import pallas as pl
from jax.experimental.pallas import tpu as pltpu
from jax.sharding import Mesh
from jax.sharding import PartitionSpec as P

D = 3584
F32 = jnp.float32
BF16 = jnp.bfloat16
MESH = pl.DeviceIdType.MESH
FSDP = ("fsdp_0", "fsdp_1")
GRP_FSDP = ("grp_0", "grp_1", "grp_2", "fsdp_0", "fsdp_1")

INBOUND = {
    "y+": ((0, 1, "m1"), (0, 1, "m2"), (0, 2, "m1"), (0, 1, "c2"), (0, 1, "c1"), (0, 2, "m2"), (0, 2, "c1"), (1, 2, "t2")),
    "y-": ((0, 3, "m1"), (0, 3, "m2"), (0, 3, "c1"), (0, 3, "c2"), (1, 3, "m2"), (0, 2, "c2"), (1, 2, "m2"), (1, 2, "c1")),
    "z+": ((1, 0, "m1"), (1, 0, "t1"), (1, 3, "m1"), (1, 1, "m1"), (1, 1, "t1"), (1, 3, "c1"), (1, 1, "c2"), (1, 2, "c2")),
    "z-": ((1, 0, "m2"), (1, 0, "c1"), (1, 0, "c2"), (1, 1, "m2"), (1, 2, "m1"), (1, 3, "c2"), (1, 1, "c1")),
    "x+": ((0, 1, "t1"), (1, 0, "t2"), (1, 3, "t1"), (0, 3, "t2"), (1, 3, "t2"), (0, 2, "t2")),
    "x-": ((0, 3, "t1"), (0, 1, "t2"), (0, 2, "t1"), (1, 1, "t2"), (1, 2, "t1")),
}
LINK_STEP = {"y+": (0, 1, 0), "y-": (0, -1, 0), "z+": (0, 0, 1), "z-": (0, 0, -1), "x+": (1, 0, 0), "x-": (-1, 0, 0)}
SWAP = {"m1": "t1", "m2": "t2", "t1": "m1", "t2": "m2"}
ROLES = ("m1", "m2", "t1", "t2", "c1", "c2")
GROUPS = {"a": ("m1", "t1"), "p": ("m2", "t2"), "q": ("c1", "c2")}
PIECE_US, HOP_US, LEAD_US, TOKENS_US = 2.48, 1.7, 2.5, 5.0


def source(link, o, d, role):
    if link == "y+":
        return (o, (d - 1) % 4, role)
    if link == "y-":
        return (o, (d + 1) % 4, role)
    if link[0] == "z":
        return (1 - o, d, role)
    return (o, d, SWAP[role])


def timeline():
    arrival = {(0, 0, role): 0.0 for role in ROLES}
    free = dict.fromkeys(INBOUND, 0.0)
    waiting = {link: list(items) for link, items in INBOUND.items()}
    events = []
    while any(waiting.values()):
        ready = [
            (max(free[link], arrival[source(link, *items[0])]), link)
            for link, items in waiting.items()
            if items and source(link, *items[0]) in arrival
        ]
        start, link = min(ready)
        item = waiting[link].pop(0)
        free[link] = start + PIECE_US
        arrival[item] = start + PIECE_US + HOP_US
        issue = max(arrival[source(link, *item)], start - LEAD_US)
        events.append((issue, 0, ("send", link, item)))
    for o in range(2):
        for d in range(4):
            for group, roles in GROUPS.items():
                when = max(TOKENS_US, *(arrival[(o, d, role)] for role in roles))
                events.append((when, 1, ("product", (o, d), group)))
    return events


def one_hot(row, first, size):
    lines = lax.broadcasted_iota(jnp.int32, (size, row.shape[1]), 0) + first
    return (lines == row).astype(F32).astype(BF16)


def across(a, b):
    return lax.dot_general(a, b, (((1,), (1,)), ((), ())), preferred_element_type=F32)


def kernel(
    tokens, target, weight, factor_a, factor_b, counts, index, totals, asel, bsel,
    tok, tgt, buf, fb, fa, cnt, idx, acc_a, acc_w, owns, picks, brow, s_part, s_recv,
    ar_c, ar_xy, ar_z, local, send_sem, recv_sem, tok_send, tok_recv, s_send, s_got, ar_send, ar_recv,
):
    zh, x, c, zl, y = (lax.axis_index(n) for n in GRP_FSDP)
    z = zh * 2 + zl
    par = lax.rem(x, 2)
    rows, depth, cands = tokens.shape[0], weight.shape[0], counts.shape[1]
    noise = 0.5 * D ** (-0.5)

    def at(dx=0, dy=0, dz=0, dc=0):
        there = lax.rem(z + dz + 8, 8)
        return (there // 2, lax.rem(x + dx + 4, 4), lax.rem(c + dc + 2, 2), lax.rem(there, 2), lax.rem(y + dy + 4, 4))

    def piece_of(role):
        return {"m1": par, "m2": 2 + par, "t1": 1 - par, "t2": 3 - par, "c1": 4, "c2": 5}[role]

    def rows_of(d):
        return pl.ds(pl.multiple_of(lax.rem(y + d, 2) * 64, 64), depth)

    def columns(start, size):
        return pl.ds(pl.multiple_of(start, 128), size)

    ar_peers = [
        [dict(dc=1)],
        [dict(dx=dx, dy=dy) for dx in range(4) for dy in range(4) if dx or dy],
        [dict(dz=dz) for dz in range(1, 8)],
    ]
    barrier = pltpu.get_barrier_semaphore()
    near = [dict(dc=1)] + [dict(dx=i) for i in (1, 3)] + [dict(dy=i) for i in (1, 3)] + [dict(dz=i) for i in (1, 7)]
    for peer in near:
        pl.semaphore_signal(barrier, inc=1, device_id=at(**peer), device_id_type=MESH)

    copies = {}

    def bring(name, src, dst):
        copies[name] = pltpu.make_async_copy(src, dst, local.at[len(copies)])
        copies[name].start()

    for role in ROLES:
        j = piece_of(role)
        if role in ("m1", "t1"):
            src = factor_a.at[:, columns(c * 256 + j * 128, 128)]
        else:
            src = weight.at[:, columns(c * 512 + (j - 2) * 128, 128)]
        bring(role, src, buf.at[0, j, rows_of(0)])
    bring("cnt", counts, cnt)
    bring("idx", index, idx)
    bring("tok", tokens, tok.at[0])
    bring("tgt", target.at[:, columns(c * 512, 512)], tgt.at[0])
    bring("fb", factor_b, fb)
    bring("fa", factor_a, fa)

    pl.semaphore_wait(barrier, len(near))

    items = [item for link in INBOUND for item in INBOUND[link]]
    sends, waited = [], set()

    def need(item):
        if item in waited:
            return
        waited.add(item)
        o, d, role = item
        if (o, d) == (0, 0):
            copies[role].wait()
            return
        k = items.index(item)
        place = buf.at[o * 4 + d, piece_of(role), rows_of(d)]
        pltpu.make_async_remote_copy(
            src_ref=place, dst_ref=place, send_sem=send_sem.at[k], recv_sem=recv_sem.at[k],
            device_id=at(dc=1), device_id_type=MESH,
        ).wait_recv()

    def send(link, item):
        so, sd, srole = source(link, *item)
        need((so, sd, srole))
        k = items.index(item)
        dx, dy, dz = LINK_STEP[link]
        j = piece_of(srole)
        copy = pltpu.make_async_remote_copy(
            src_ref=buf.at[so * 4 + sd, j, rows_of(sd)],
            dst_ref=buf.at[item[0] * 4 + item[1], j, rows_of(sd)],
            send_sem=send_sem.at[k], recv_sem=recv_sem.at[k],
            device_id=at(-dx, -dy, -dz), device_id_type=MESH,
        )
        copy.start()
        sends.append(copy)

    swaps = [
        pltpu.make_async_remote_copy(
            src_ref=src, dst_ref=dst, send_sem=tok_send.at[k], recv_sem=tok_recv.at[k],
            device_id=at(dc=1), device_id_type=MESH,
        )
        for k, (src, dst) in enumerate(
            ((tokens, tok.at[1]), (target.at[:, columns((1 - c) * 512, 512)], tgt.at[1]))
        )
    ]

    def start_swaps():
        for copy in swaps:
            copy.start()

    def clear():
        zero = jnp.zeros((64, 128), BF16)
        for d in range(4):
            gap = pl.multiple_of((1 - lax.rem(y + d, 2)) * depth, 64)
            for o in range(2):
                for j in range(6):
                    buf[o * 4 + d, j, pl.ds(gap, 64), :] = zero

    def owners():
        copies["cnt"].wait()
        copies["idx"].wait()
        count = cnt[...]
        upto = (
            lax.broadcasted_iota(jnp.int32, (cands, cands), 0) <= lax.broadcasted_iota(jnp.int32, (cands, cands), 1)
        ).astype(F32).astype(BF16)
        high = jnp.broadcast_to((count >> 7).astype(F32), (16, cands)).astype(BF16)
        low = jnp.broadcast_to((count & 127).astype(F32), (16, cands)).astype(BF16)
        ends = jnp.dot(high, upto, preferred_element_type=F32) * 128.0 + jnp.dot(
            low, upto, preferred_element_type=F32
        )
        ends = ends[0:1, :].astype(jnp.int32)
        starts = ends - count
        for i in range(2):
            who = lax.rem(c + i, 2)
            block = ((zh * 4 + x) * 2 + who) * 8 + zl * 4 + y
            token = lax.broadcasted_iota(jnp.int32, (rows, cands), 0) + block * rows
            owns[i] = ((starts <= token) & (token < ends)).astype(F32).astype(BF16)

    def left_picks():
        left = one_hot(idx[0:1, :], c * 256, 256)
        for i in range(2):
            picks[i] = across(owns[i], left)

    def right_rows():
        copies["fb"].wait()
        right = one_hot(idx[1:2, :], 0, fb.shape[0])
        mine = fb[:, columns(c * 512, 512)]
        for i in range(2):
            chosen = across(owns[i], right).astype(BF16)
            brow[i] = jnp.dot(chosen, mine, preferred_element_type=F32)

    def chosen_left():
        copies["fa"].wait()
        left = one_hot(idx[0:1, :], 0, fa.shape[1])
        asel[...] = jnp.dot(fa[...], left, preferred_element_type=F32).astype(BF16)

    def chosen_right():
        size = (cands, cands)
        line, lane = lax.broadcasted_iota(jnp.int32, size, 0), lax.broadcasted_iota(jnp.int32, size, 1)
        row = idx[1:2, :].astype(F32)
        column = jnp.sum(jnp.where(line == lane, row, 0.0), axis=1, keepdims=True)
        right = (column == lane.astype(F32)).astype(F32).astype(BF16)
        bsel[...] = jnp.dot(right, fb[...], preferred_element_type=F32).astype(BF16)

    seen, left_over = set(), {"a": 8}
    s_copies = [
        pltpu.make_async_remote_copy(
            src_ref=s_part.at[i], dst_ref=s_recv.at[1 - i], send_sem=s_send.at[i], recv_sem=s_got.at[i],
            device_id=at(dc=1), device_id_type=MESH,
        )
        for i in range(2)
    ]

    def product(slot, group):
        o, d = slot
        for role in GROUPS[group]:
            need((o, d, role))
        first = lax.rem(zl + o, 2) * 4 + lax.rem(y + d, 4)
        window = columns(first // 2 * 896 + lax.rem(first, 2) * 384, 512)
        j = "apq".index(group) * 2
        block = jnp.concatenate([buf[o * 4 + d, j], buf[o * 4 + d, j + 1]], axis=1)
        acc, lanes = (acc_a, slice(0, 256)) if group == "a" else (acc_w, slice(j * 128 - 256, j * 128))
        for i in range(2):
            if i == 0 and "tok" not in waited:
                copies["tok"].wait()
            if i == 1 and "tok" not in waited:
                swaps[0].wait_recv()
                waited.add("tok")
            part = jnp.dot(tok[i, :, window], block, preferred_element_type=F32)
            if group in seen:
                acc[i, :, lanes] += part
            else:
                acc[i, :, lanes] = part
        seen.add(group)
        if group == "a":
            left_over["a"] -= 1
            if left_over["a"] == 0:
                for i in range(2):
                    kept = jnp.where(picks[i] > 0.5, acc_a[i], 0.0)
                    s_part[i] = kept[:, :128] + kept[:, 128:]
                    s_copies[i].start()

    def perturb():
        copies["tgt"].wait()
        swaps[1].wait_recv()
        for copy in s_copies:
            copy.wait_recv()
        for i in range(2):
            score = jnp.sum(s_part[i] + s_recv[i], axis=1, keepdims=True) * noise
            acc_w[i] += score * brow[i] - tgt[i].astype(F32)

    events = timeline()
    after_a = max(when for when, _, what in events if what[0] == "product" and what[2] == "a")
    events += [
        (0.05, 2, (start_swaps,)), (0.1, 2, (clear,)), (0.5, 2, (owners,)), (1.0, 2, (left_picks,)), (1.5, 2, (right_rows,)),
        (2.0, 2, (chosen_left,)), (2.5, 2, (chosen_right,)), (after_a + 1.2, 2, (perturb,)),
    ]
    for _, _, what in sorted(events, key=lambda event: event[:2]):
        if what[0] == "send":
            send(*what[1:])
        elif what[0] == "product":
            product(*what[1:])
        else:
            what[0]()

    total = jnp.zeros((1, cands), F32)
    for i in range(2):
        diff = acc_w[i]
        square = diff * diff
        square = (square[:, :128] + square[:, 128:256]) + (square[:, 256:384] + square[:, 384:])
        loss = jnp.sum(square, axis=1, keepdims=True) * (1.0 / 1024)
        total += jnp.sum(owns[i].astype(F32) * loss, axis=0, keepdims=True)
    first = 0
    for group, ring, me, number in (
        (ar_peers[0], ar_c, c, lambda dc: 1 - c),
        (ar_peers[1], ar_xy, x * 4 + y, lambda dx, dy: lax.rem(x - dx + 4, 4) * 4 + lax.rem(y - dy + 4, 4)),
        (ar_peers[2], ar_z, z, lambda dz: lax.rem(z - dz + 8, 8)),
    ):
        ring[me] = total
        out = [
            pltpu.make_async_remote_copy(
                src_ref=ring.at[me], dst_ref=ring.at[me], send_sem=ar_send.at[first + k], recv_sem=ar_recv.at[first + k],
                device_id=at(**peer), device_id_type=MESH,
            )
            for k, peer in enumerate(group)
        ]
        for copy in out:
            copy.start()
        for k, peer in enumerate(group):
            place = ring.at[number(**peer)]
            pltpu.make_async_remote_copy(
                src_ref=place, dst_ref=place, send_sem=ar_send.at[first + k], recv_sem=ar_recv.at[first + k],
                device_id=at(**peer), device_id_type=MESH,
            ).wait_recv()
        total = ring[0]
        for k in range(1, ring.shape[0]):
            total += ring[k]
        sends.extend(out)
        first += len(group)
    totals[...] = total
    for copy in sends + swaps + s_copies:
        copy.wait_send()


def gather_and_sum(tokens, target, weight, factor_a, factor_b, counts, index):
    rows, depth = tokens.shape[0], weight.shape[0]
    cands, pool, out = counts.shape[1], factor_a.shape[1], weight.shape[1]
    links = sum(map(len, INBOUND.values()))
    dma = pltpu.SemaphoreType.DMA
    return pl.pallas_call(
        kernel,
        name="gather_and_sum",
        out_shape=(
            jax.ShapeDtypeStruct((1, cands), F32),
            jax.ShapeDtypeStruct((depth, cands), BF16),
            jax.ShapeDtypeStruct((cands, out), BF16),
        ),
        in_specs=[pl.BlockSpec(memory_space=pltpu.HBM)] * 7,
        out_specs=(pl.BlockSpec(memory_space=pltpu.VMEM),) * 3,
        scratch_shapes=[
            pltpu.VMEM((2, rows, D), BF16),
            pltpu.VMEM((2, rows, out // 2), BF16),
            pltpu.VMEM((8, 6, depth + 64, 128), BF16),
            pltpu.VMEM((pool, out), BF16),
            pltpu.VMEM((depth, pool), BF16),
            pltpu.VMEM((1, cands), jnp.int32),
            pltpu.VMEM((2, cands), jnp.int32),
            pltpu.VMEM((2, rows, pool // 2), F32),
            pltpu.VMEM((2, rows, out // 2), F32),
            pltpu.VMEM((2, rows, cands), BF16),
            pltpu.VMEM((2, rows, pool // 2), F32),
            pltpu.VMEM((2, rows, out // 2), F32),
            pltpu.VMEM((2, rows, 128), F32),
            pltpu.VMEM((2, rows, 128), F32),
            pltpu.VMEM((2, 1, cands), F32),
            pltpu.VMEM((16, 1, cands), F32),
            pltpu.VMEM((8, 1, cands), F32),
            dma((12,)),
            dma((links,)),
            dma((links,)),
            dma((2,)),
            dma((2,)),
            dma((2,)),
            dma((2,)),
            dma((23,)),
            dma((23,)),
        ],
        compiler_params=pltpu.CompilerParams(collective_id=0, has_side_effects=True, vmem_limit_bytes=40 << 20),
    )(*(pltpu.with_memory_space_constraint(a, pltpu.HBM) for a in (tokens, target, weight, factor_a, factor_b, counts, index)))


def finish_kernel(totals, counts, asel, bsel, update, scores, block, sem):
    cands, steps = counts.shape[1], block.shape[0]
    size = block.shape[1]
    fitness = -totals[...] / counts[...].astype(F32)
    middle = jnp.mean(fitness, axis=1, keepdims=True)
    spread = jnp.mean((fitness - middle) ** 2, axis=1, keepdims=True)
    score = (fitness - middle) / jnp.sqrt(spread + 1e-06)
    scores[...] = score
    out = []
    for k in range(steps):
        lines = slice(k * size, (k + 1) * size)
        scaled = (asel[lines, :].astype(F32) * score).astype(BF16)
        block[k] = jnp.dot(scaled, bsel[...], preferred_element_type=F32) * (cands**-0.5)
        copy = pltpu.make_async_copy(block.at[k], update.at[lines, :], sem.at[k])
        copy.start()
        out.append(copy)
    for copy in out:
        copy.wait()


def finish(totals, counts, asel, bsel):
    depth, cands = asel.shape
    out = bsel.shape[1]
    steps = 4
    vmem = pl.BlockSpec(memory_space=pltpu.VMEM)
    return pl.pallas_call(
        finish_kernel,
        name="finish",
        out_shape=(jax.ShapeDtypeStruct((depth, out), F32), jax.ShapeDtypeStruct((1, cands), F32)),
        in_specs=[vmem] * 4,
        out_specs=(pl.BlockSpec(memory_space=pltpu.HBM), vmem),
        scratch_shapes=[pltpu.VMEM((steps, depth // steps, out), F32), pltpu.SemaphoreType.DMA((steps,))],
        compiler_params=pltpu.CompilerParams(vmem_limit_bytes=16 << 20),
    )(totals, counts, asel, bsel)


def per_device(tokens, target, weight, factor_a, factor_b, counts, cand_index):
    counts = counts.reshape(1, -1)
    totals, asel, bsel = gather_and_sum(tokens, target, weight, factor_a, factor_b, counts, cand_index.T)
    update, scores = finish(totals, counts, asel, bsel)
    return (update, scores.reshape(-1))


def solution(mesh):
    split = Mesh(mesh.devices.reshape(4, 4, 2, 2, 4), GRP_FSDP)
    placed = (P(GRP_FSDP, None), P(GRP_FSDP, None), P(FSDP, None), P(FSDP, None), P(), P(), P())
    return jax.shard_map(
        per_device, mesh=split, in_specs=placed, out_specs=(P(FSDP, None), P()), check_vma=False
    )
```

```python
import functools

import jax
import jax.numpy as jnp
from jax import lax
from jax.experimental import pallas as pl
from jax.experimental.pallas import tpu as pltpu
from jax.sharding import Mesh
from jax.sharding import PartitionSpec as P

D = 3584
F32 = jnp.float32
BF16 = jnp.bfloat16
MESH = pl.DeviceIdType.MESH
FSDP = ("fsdp_0", "fsdp_1")
GRP_FSDP = ("grp_0", "grp_1", "grp_2", "fsdp_0", "fsdp_1")

INBOUND = {
    "y+": (
        (0, 1, "m1", 0), (0, 1, "m1", 1), (0, 1, "m2", 0), (0, 1, "m2", 1), (0, 2, "m1", 1), (0, 2, "m1", 0),
        (0, 2, "m2", 0), (0, 1, "c2", 1), (0, 1, "c1", 1), (0, 1, "c1", 0), (0, 1, "c2", 0), (1, 1, "c1", 1),
        (1, 1, "c2", 1), (0, 2, "c2", 1), (1, 2, "c1", 1),
    ),
    "y-": (
        (0, 3, "m1", 0), (0, 3, "m1", 1), (0, 3, "m2", 1), (0, 3, "m2", 0), (1, 3, "m1", 1), (0, 2, "m2", 1),
        (0, 3, "c2", 1), (0, 3, "c2", 0), (0, 3, "c1", 0), (0, 3, "c1", 1), (0, 2, "c2", 0), (0, 2, "c1", 0),
        (1, 3, "c1", 1), (0, 2, "c1", 1), (1, 2, "c2", 1),
    ),
    "z+": (
        (1, 0, "m1", 0), (1, 0, "m2", 0), (1, 0, "t1", 0), (1, 1, "m1", 0), (1, 1, "m1", 1), (1, 0, "c2", 0),
        (1, 0, "c1", 0), (1, 1, "m2", 0), (1, 3, "m2", 0), (1, 2, "m1", 0), (1, 2, "m2", 0), (1, 2, "m2", 1),
        (1, 3, "c2", 0), (1, 1, "c2", 0), (1, 2, "c2", 0),
    ),
    "z-": (
        (1, 0, "m1", 1), (1, 0, "m2", 1), (1, 0, "t1", 1), (1, 3, "m1", 0), (1, 0, "c1", 1), (1, 0, "c2", 1),
        (1, 1, "m2", 1), (1, 3, "m2", 1), (1, 0, "t2", 0), (1, 2, "m1", 1), (1, 3, "c2", 1), (1, 3, "c1", 0),
        (1, 2, "t1", 0), (1, 1, "c1", 0), (1, 2, "c1", 0),
    ),
    "x+": (
        (0, 3, "t1", 0), (0, 1, "t1", 1), (0, 1, "t2", 0), (0, 3, "t2", 1), (1, 1, "t1", 1), (0, 1, "t2", 1),
        (1, 1, "t1", 0), (0, 2, "t1", 0), (1, 1, "t2", 0), (0, 2, "t2", 1), (0, 2, "t2", 0), (1, 2, "t2", 0),
    ),
    "x-": (
        (0, 1, "t1", 0), (0, 3, "t1", 1), (1, 0, "t2", 1), (0, 3, "t2", 0), (1, 3, "t1", 0), (0, 2, "t1", 1),
        (1, 3, "t1", 1), (1, 3, "t2", 1), (1, 1, "t2", 1), (1, 3, "t2", 0), (1, 2, "t1", 1), (1, 2, "t2", 1),
    ),
}
LINK_STEP = {"y+": (0, 1, 0), "y-": (0, -1, 0), "z+": (0, 0, 1), "z-": (0, 0, -1), "x+": (1, 0, 0), "x-": (-1, 0, 0)}
SWAP = {"m1": "t1", "m2": "t2", "t1": "m1", "t2": "m2"}
ROLES = ("m1", "m2", "t1", "t2", "c1", "c2")
GROUPS = {"a": ("m1", "t1"), "p": ("m2", "t2"), "q": ("c1", "c2")}
PARTS = 2
PIECE_US, HOP_US, LEAD_US, TOKENS_US, LATE_US = 2.48 / PARTS, 1.7, 1.25, 5.0, 1.5


def source(link, o, d, role, part):
    if link == "y+":
        return (o, (d - 1) % 4, role, part)
    if link == "y-":
        return (o, (d + 1) % 4, role, part)
    if link[0] == "z":
        return (1 - o, d, role, part)
    return (o, d, SWAP[role], part)


def timeline():
    arrival = {(0, 0, role, part): 0.0 for role in ROLES for part in range(PARTS)}
    free = dict.fromkeys(INBOUND, 0.0)
    waiting = {link: list(items) for link, items in INBOUND.items()}
    events = []
    while any(waiting.values()):
        ready = [
            (max(free[link], arrival[source(link, *items[0])]), link)
            for link, items in waiting.items()
            if items and source(link, *items[0]) in arrival
        ]
        start, link = min(ready)
        item = waiting[link].pop(0)
        free[link] = start + PIECE_US
        arrival[item] = start + PIECE_US + HOP_US
        issue = max(arrival[source(link, *item)], start - LEAD_US)
        events.append((issue, 0, ("send", link, item)))
    for o in range(2):
        for d in range(4):
            for group, roles in GROUPS.items():
                when = max(TOKENS_US, *(arrival[(o, d, role, part)] for role in roles for part in range(PARTS)))
                events.append((when + LATE_US, 1, ("product", (o, d), group)))
    return events


def one_hot(row, first, size):
    lines = lax.broadcasted_iota(jnp.int32, (size, row.shape[1]), 0) + first
    return (lines == row).astype(F32).astype(BF16)


def across(a, b):
    return lax.dot_general(a, b, (((1,), (1,)), ((), ())), preferred_element_type=F32)


def kernel(
    tokens, target, weight, factor_a, factor_b, counts, index, totals, asel, bsel,
    tok, tgt, buf, fb, fa, cnt, idx, acc_a, acc_w, owns, picks, brow, s_part, s_recv,
    ar_c, ar_xy, ar_z, local, send_sem, recv_sem, tok_send, tok_recv, s_send, s_got, ar_send, ar_recv,
):
    zh, x, c, zl, y = (lax.axis_index(n) for n in GRP_FSDP)
    z = zh * 2 + zl
    par = lax.rem(x, 2)
    rows, depth, cands = tokens.shape[0], weight.shape[0], counts.shape[1]
    noise = 0.5 * D ** (-0.5)

    def at(dx=0, dy=0, dz=0, dc=0):
        there = lax.rem(z + dz + 8, 8)
        return (there // 2, lax.rem(x + dx + 4, 4), lax.rem(c + dc + 2, 2), lax.rem(there, 2), lax.rem(y + dy + 4, 4))

    def piece_of(role):
        return {"m1": par, "m2": 2 + par, "t1": 1 - par, "t2": 3 - par, "c1": 4, "c2": 5}[role]

    def rows_of(d, part=0, parts=1):
        size = depth // parts
        return pl.ds(pl.multiple_of(lax.rem(y + d, 2) * 64 + part * size, 32), size)

    def columns(start, size):
        return pl.ds(pl.multiple_of(start, 128), size)

    ar_peers = [
        [dict(dc=1)],
        [dict(dx=dx, dy=dy) for dx in range(4) for dy in range(4) if dx or dy],
        [dict(dz=dz) for dz in range(1, 8)],
    ]
    barrier = pltpu.get_barrier_semaphore()
    near = [dict(dc=1)] + [dict(dx=i) for i in (1, 3)] + [dict(dy=i) for i in (1, 3)] + [dict(dz=i) for i in (1, 7)]
    for peer in near:
        pl.semaphore_signal(barrier, inc=1, device_id=at(**peer), device_id_type=MESH)

    copies = {}

    def bring(name, src, dst):
        copies[name] = pltpu.make_async_copy(src, dst, local.at[len(copies)])
        copies[name].start()

    for role in ROLES:
        j = piece_of(role)
        if role in ("m1", "t1"):
            src = factor_a.at[:, columns(c * 256 + j * 128, 128)]
        else:
            src = weight.at[:, columns(c * 512 + (j - 2) * 128, 128)]
        bring(role, src, buf.at[0, j, rows_of(0)])
    bring("cnt", counts, cnt)
    bring("idx", index, idx)
    bring("tok", tokens, tok.at[0])
    bring("tgt", target.at[:, columns(c * 512, 512)], tgt.at[0])
    bring("fb", factor_b, fb)
    bring("fa", factor_a, fa)

    pl.semaphore_wait(barrier, len(near))

    items = [item for link in INBOUND for item in INBOUND[link]]
    sends, waited = [], set()

    def need(item):
        if item in waited:
            return
        waited.add(item)
        o, d, role, part = item
        if (o, d) == (0, 0):
            if part == 0:
                copies[role].wait()
            return
        k = items.index(item)
        place = buf.at[o * 4 + d, piece_of(role), rows_of(d, part, PARTS)]
        pltpu.make_async_remote_copy(
            src_ref=place, dst_ref=place, send_sem=send_sem.at[k], recv_sem=recv_sem.at[k],
            device_id=at(dc=1), device_id_type=MESH,
        ).wait_recv()

    def send(link, item):
        so, sd, srole, part = source(link, *item)
        need((so, sd, srole, 0 if (so, sd) == (0, 0) else part))
        k = items.index(item)
        dx, dy, dz = LINK_STEP[link]
        j = piece_of(srole)
        copy = pltpu.make_async_remote_copy(
            src_ref=buf.at[so * 4 + sd, j, rows_of(sd, part, PARTS)],
            dst_ref=buf.at[item[0] * 4 + item[1], j, rows_of(sd, part, PARTS)],
            send_sem=send_sem.at[k], recv_sem=recv_sem.at[k],
            device_id=at(-dx, -dy, -dz), device_id_type=MESH,
        )
        copy.start()
        sends.append(copy)

    swaps = [
        pltpu.make_async_remote_copy(
            src_ref=src, dst_ref=dst, send_sem=tok_send.at[k], recv_sem=tok_recv.at[k],
            device_id=at(dc=1), device_id_type=MESH,
        )
        for k, (src, dst) in enumerate(
            ((tokens, tok.at[1]), (target.at[:, columns((1 - c) * 512, 512)], tgt.at[1]))
        )
    ]

    def start_swaps():
        for copy in swaps:
            copy.start()

    def clear():
        zero = jnp.zeros((64, 128), BF16)
        for d in range(4):
            gap = pl.multiple_of((1 - lax.rem(y + d, 2)) * depth, 64)
            for o in range(2):
                for j in range(6):
                    buf[o * 4 + d, j, pl.ds(gap, 64), :] = zero

    def owners():
        copies["cnt"].wait()
        copies["idx"].wait()
        count = cnt[...]
        upto = (
            lax.broadcasted_iota(jnp.int32, (cands, cands), 0) <= lax.broadcasted_iota(jnp.int32, (cands, cands), 1)
        ).astype(F32).astype(BF16)
        high = jnp.broadcast_to((count >> 7).astype(F32), (16, cands)).astype(BF16)
        low = jnp.broadcast_to((count & 127).astype(F32), (16, cands)).astype(BF16)
        ends = jnp.dot(high, upto, preferred_element_type=F32) * 128.0 + jnp.dot(
            low, upto, preferred_element_type=F32
        )
        ends = ends[0:1, :].astype(jnp.int32)
        starts = ends - count
        for i in range(2):
            who = lax.rem(c + i, 2)
            block = ((zh * 4 + x) * 2 + who) * 8 + zl * 4 + y
            token = lax.broadcasted_iota(jnp.int32, (rows, cands), 0) + block * rows
            owns[i] = ((starts <= token) & (token < ends)).astype(F32).astype(BF16)

    def left_picks():
        left = one_hot(idx[0:1, :], c * 256, 256)
        for i in range(2):
            picks[i] = across(owns[i], left)

    def right_rows():
        copies["fb"].wait()
        right = one_hot(idx[1:2, :], 0, fb.shape[0])
        mine = fb[:, columns(c * 512, 512)]
        for i in range(2):
            chosen = across(owns[i], right).astype(BF16)
            brow[i] = jnp.dot(chosen, mine, preferred_element_type=F32)

    def chosen_left():
        copies["fa"].wait()
        left = one_hot(idx[0:1, :], 0, fa.shape[1])
        asel[...] = jnp.dot(fa[...], left, preferred_element_type=F32).astype(BF16)

    def chosen_right():
        size = (cands, cands)
        line, lane = lax.broadcasted_iota(jnp.int32, size, 0), lax.broadcasted_iota(jnp.int32, size, 1)
        row = idx[1:2, :].astype(F32)
        column = jnp.sum(jnp.where(line == lane, row, 0.0), axis=1, keepdims=True)
        right = (column == lane.astype(F32)).astype(F32).astype(BF16)
        bsel[...] = jnp.dot(right, fb[...], preferred_element_type=F32).astype(BF16)

    seen, left_over = set(), {"a": 8}
    s_copies = [
        pltpu.make_async_remote_copy(
            src_ref=s_part.at[i], dst_ref=s_recv.at[1 - i], send_sem=s_send.at[i], recv_sem=s_got.at[i],
            device_id=at(dc=1), device_id_type=MESH,
        )
        for i in range(2)
    ]

    def product(slot, group):
        o, d = slot
        for role in GROUPS[group]:
            for part in range(PARTS):
                need((o, d, role, part))
        first = lax.rem(zl + o, 2) * 4 + lax.rem(y + d, 4)
        window = columns(first // 2 * 896 + lax.rem(first, 2) * 384, 512)
        j = "apq".index(group) * 2
        block = jnp.concatenate([buf[o * 4 + d, j], buf[o * 4 + d, j + 1]], axis=1)
        acc, lanes = (acc_a, slice(0, 256)) if group == "a" else (acc_w, slice(j * 128 - 256, j * 128))
        for i in range(2):
            if i == 0 and "tok" not in waited:
                copies["tok"].wait()
            if i == 1 and "tok" not in waited:
                swaps[0].wait_recv()
                waited.add("tok")
            part = jnp.dot(tok[i, :, window], block, preferred_element_type=F32)
            if group in seen:
                acc[i, :, lanes] += part
            else:
                acc[i, :, lanes] = part
        seen.add(group)
        if group == "a":
            left_over["a"] -= 1
            if left_over["a"] == 0:
                for i in range(2):
                    kept = jnp.where(picks[i] > 0.5, acc_a[i], 0.0)
                    s_part[i] = kept[:, :128] + kept[:, 128:]
                    s_copies[i].start()

    def perturb():
        copies["tgt"].wait()
        swaps[1].wait_recv()
        for copy in s_copies:
            copy.wait_recv()
        for i in range(2):
            score = jnp.sum(s_part[i] + s_recv[i], axis=1, keepdims=True) * noise
            acc_w[i] += score * brow[i] - tgt[i].astype(F32)

    events = timeline()
    after_a = max(when for when, _, what in events if what[0] == "product" and what[2] == "a")
    events += [
        (0.05, 2, (start_swaps,)), (0.1, 2, (clear,)), (0.5, 2, (owners,)), (1.0, 2, (left_picks,)), (1.5, 2, (right_rows,)),
        (after_a + 1.2, 2, (perturb,)),
    ]
    for _, _, what in sorted(events, key=lambda event: event[:2]):
        if what[0] == "send":
            send(*what[1:])
        elif what[0] == "product":
            product(*what[1:])
        else:
            what[0]()

    total = jnp.zeros((1, cands), F32)
    for i in range(2):
        diff = acc_w[i]
        square = diff * diff
        square = (square[:, :128] + square[:, 128:256]) + (square[:, 256:384] + square[:, 384:])
        loss = jnp.sum(square, axis=1, keepdims=True) * (1.0 / 1024)
        total += jnp.sum(owns[i].astype(F32) * loss, axis=0, keepdims=True)
    first = 0
    for group, ring, me, number in (
        (ar_peers[0], ar_c, c, lambda dc: 1 - c),
        (ar_peers[1], ar_xy, x * 4 + y, lambda dx, dy: lax.rem(x - dx + 4, 4) * 4 + lax.rem(y - dy + 4, 4)),
        (ar_peers[2], ar_z, z, lambda dz: lax.rem(z - dz + 8, 8)),
    ):
        ring[me] = total
        out = [
            pltpu.make_async_remote_copy(
                src_ref=ring.at[me], dst_ref=ring.at[me], send_sem=ar_send.at[first + k], recv_sem=ar_recv.at[first + k],
                device_id=at(**peer), device_id_type=MESH,
            )
            for k, peer in enumerate(group)
        ]
        for copy in out:
            copy.start()
        if group is ar_peers[1]:
            chosen_left()
            chosen_right()
        for k, peer in enumerate(group):
            place = ring.at[number(**peer)]
            pltpu.make_async_remote_copy(
                src_ref=place, dst_ref=place, send_sem=ar_send.at[first + k], recv_sem=ar_recv.at[first + k],
                device_id=at(**peer), device_id_type=MESH,
            ).wait_recv()
        total = ring[0]
        for k in range(1, ring.shape[0]):
            total += ring[k]
        sends.extend(out)
        first += len(group)
    totals[...] = total
    for copy in sends + swaps + s_copies:
        copy.wait_send()


def gather_and_sum(tokens, target, weight, factor_a, factor_b, counts, index):
    rows, depth = tokens.shape[0], weight.shape[0]
    cands, pool, out = counts.shape[1], factor_a.shape[1], weight.shape[1]
    links = sum(map(len, INBOUND.values()))
    dma = pltpu.SemaphoreType.DMA
    return pl.pallas_call(
        kernel,
        name="gather_and_sum",
        out_shape=(
            jax.ShapeDtypeStruct((1, cands), F32),
            jax.ShapeDtypeStruct((depth, cands), BF16),
            jax.ShapeDtypeStruct((cands, out), BF16),
        ),
        in_specs=[pl.BlockSpec(memory_space=pltpu.HBM)] * 7,
        out_specs=(pl.BlockSpec(memory_space=pltpu.VMEM),) * 3,
        scratch_shapes=[
            pltpu.VMEM((2, rows, D), BF16),
            pltpu.VMEM((2, rows, out // 2), BF16),
            pltpu.VMEM((8, 6, depth + 64, 128), BF16),
            pltpu.VMEM((pool, out), BF16),
            pltpu.VMEM((depth, pool), BF16),
            pltpu.VMEM((1, cands), jnp.int32),
            pltpu.VMEM((2, cands), jnp.int32),
            pltpu.VMEM((2, rows, pool // 2), F32),
            pltpu.VMEM((2, rows, out // 2), F32),
            pltpu.VMEM((2, rows, cands), BF16),
            pltpu.VMEM((2, rows, pool // 2), F32),
            pltpu.VMEM((2, rows, out // 2), F32),
            pltpu.VMEM((2, rows, 128), F32),
            pltpu.VMEM((2, rows, 128), F32),
            pltpu.VMEM((2, 1, cands), F32),
            pltpu.VMEM((16, 1, cands), F32),
            pltpu.VMEM((8, 1, cands), F32),
            dma((12,)),
            dma((links,)),
            dma((links,)),
            dma((2,)),
            dma((2,)),
            dma((2,)),
            dma((2,)),
            dma((23,)),
            dma((23,)),
        ],
        compiler_params=pltpu.CompilerParams(collective_id=0, has_side_effects=True, vmem_limit_bytes=40 << 20),
    )(*(pltpu.with_memory_space_constraint(a, pltpu.HBM) for a in (tokens, target, weight, factor_a, factor_b, counts, index)))


def finish_kernel(totals, counts, asel, bsel, update, scores, block, sem):
    cands, steps = counts.shape[1], block.shape[0]
    size = block.shape[1]
    fitness = -totals[...] / counts[...].astype(F32)
    middle = jnp.mean(fitness, axis=1, keepdims=True)
    spread = jnp.mean((fitness - middle) ** 2, axis=1, keepdims=True)
    score = (fitness - middle) / jnp.sqrt(spread + 1e-06)
    scores[...] = score
    out = []
    for k in range(steps):
        lines = slice(k * size, (k + 1) * size)
        scaled = (asel[lines, :].astype(F32) * score).astype(BF16)
        block[k] = jnp.dot(scaled, bsel[...], preferred_element_type=F32) * (cands**-0.5)
        copy = pltpu.make_async_copy(block.at[k], update.at[lines, :], sem.at[k])
        copy.start()
        out.append(copy)
    for copy in out:
        copy.wait()


def finish(totals, counts, asel, bsel):
    depth, cands = asel.shape
    out = bsel.shape[1]
    steps = 4
    vmem = pl.BlockSpec(memory_space=pltpu.VMEM)
    return pl.pallas_call(
        finish_kernel,
        name="finish",
        out_shape=(jax.ShapeDtypeStruct((depth, out), F32), jax.ShapeDtypeStruct((1, cands), F32)),
        in_specs=[vmem] * 4,
        out_specs=(pl.BlockSpec(memory_space=pltpu.HBM), vmem),
        scratch_shapes=[pltpu.VMEM((steps, depth // steps, out), F32), pltpu.SemaphoreType.DMA((steps,))],
        compiler_params=pltpu.CompilerParams(vmem_limit_bytes=16 << 20),
    )(totals, counts, asel, bsel)


def per_device(tokens, target, weight, factor_a, factor_b, counts, cand_index):
    counts = counts.reshape(1, -1)
    totals, asel, bsel = gather_and_sum(tokens, target, weight, factor_a, factor_b, counts, cand_index.T)
    update, scores = finish(totals, counts, asel, bsel)
    return (update, scores.reshape(-1))


def solution(mesh):
    split = Mesh(mesh.devices.reshape(4, 4, 2, 2, 4), GRP_FSDP)
    placed = (P(GRP_FSDP, None), P(GRP_FSDP, None), P(FSDP, None), P(FSDP, None), P(), P(), P())
    return jax.shard_map(
        per_device, mesh=split, in_specs=placed, out_specs=(P(FSDP, None), P()), check_vma=False
    )
```

```python
import functools

import jax
import jax.numpy as jnp
from jax import lax
from jax.experimental import pallas as pl
from jax.experimental.pallas import tpu as pltpu
from jax.sharding import Mesh
from jax.sharding import PartitionSpec as P

D = 3584
F32 = jnp.float32
BF16 = jnp.bfloat16
MESH = pl.DeviceIdType.MESH
FSDP = ("fsdp_0", "fsdp_1")
GRP_FSDP = ("grp_0", "grp_1", "grp_2", "fsdp_0", "fsdp_1")

INBOUND = {
    "y+": (
        (0, 1, "m1", 0), (0, 1, "m1", 1), (0, 1, "m2", 0), (0, 1, "m2", 1), (0, 2, "m1", 1), (0, 2, "m1", 0),
        (0, 2, "m2", 0), (0, 1, "c2", 1), (0, 1, "c1", 1), (0, 1, "c1", 0), (0, 1, "c2", 0), (1, 1, "c1", 1),
        (1, 1, "c2", 1), (0, 2, "c2", 1), (1, 2, "c1", 1),
    ),
    "y-": (
        (0, 3, "m1", 0), (0, 3, "m1", 1), (0, 3, "m2", 1), (0, 3, "m2", 0), (1, 3, "m1", 1), (0, 2, "m2", 1),
        (0, 3, "c2", 1), (0, 3, "c2", 0), (0, 3, "c1", 0), (0, 3, "c1", 1), (0, 2, "c2", 0), (0, 2, "c1", 0),
        (1, 3, "c1", 1), (0, 2, "c1", 1), (1, 2, "c2", 1),
    ),
    "z+": (
        (1, 0, "m1", 0), (1, 0, "m2", 0), (1, 0, "t1", 0), (1, 1, "m1", 0), (1, 1, "m1", 1), (1, 0, "c2", 0),
        (1, 0, "c1", 0), (1, 1, "m2", 0), (1, 3, "m2", 0), (1, 2, "m1", 0), (1, 2, "m2", 0), (1, 2, "m2", 1),
        (1, 3, "c2", 0), (1, 1, "c2", 0), (1, 2, "c2", 0),
    ),
    "z-": (
        (1, 0, "m1", 1), (1, 0, "m2", 1), (1, 0, "t1", 1), (1, 3, "m1", 0), (1, 0, "c1", 1), (1, 0, "c2", 1),
        (1, 1, "m2", 1), (1, 3, "m2", 1), (1, 0, "t2", 0), (1, 2, "m1", 1), (1, 3, "c2", 1), (1, 3, "c1", 0),
        (1, 2, "t1", 0), (1, 1, "c1", 0), (1, 2, "c1", 0),
    ),
    "x+": (
        (0, 3, "t1", 0), (0, 1, "t1", 1), (0, 1, "t2", 0), (0, 3, "t2", 1), (1, 1, "t1", 1), (0, 1, "t2", 1),
        (1, 1, "t1", 0), (0, 2, "t1", 0), (1, 1, "t2", 0), (0, 2, "t2", 1), (0, 2, "t2", 0), (1, 2, "t2", 0),
    ),
    "x-": (
        (0, 1, "t1", 0), (0, 3, "t1", 1), (1, 0, "t2", 1), (0, 3, "t2", 0), (1, 3, "t1", 0), (0, 2, "t1", 1),
        (1, 3, "t1", 1), (1, 3, "t2", 1), (1, 1, "t2", 1), (1, 3, "t2", 0), (1, 2, "t1", 1), (1, 2, "t2", 1),
    ),
}
LINK_STEP = {"y+": (0, 1, 0), "y-": (0, -1, 0), "z+": (0, 0, 1), "z-": (0, 0, -1), "x+": (1, 0, 0), "x-": (-1, 0, 0)}
SWAP = {"m1": "t1", "m2": "t2", "t1": "m1", "t2": "m2"}
ROLES = ("m1", "m2", "t1", "t2", "c1", "c2")
GROUPS = {"a": ("m1", "t1"), "p": ("m2", "t2"), "q": ("c1", "c2")}
PARTS = 2
PIECE_US, HOP_US, LEAD_US, TOKENS_US, LATE_US = 2.48 / PARTS, 1.7, 1.25, 5.0, 1.5


def source(link, o, d, role, part):
    if link == "y+":
        return (o, (d - 1) % 4, role, part)
    if link == "y-":
        return (o, (d + 1) % 4, role, part)
    if link[0] == "z":
        return (1 - o, d, role, part)
    return (o, d, SWAP[role], part)


def timeline():
    arrival = {(0, 0, role, part): 0.0 for role in ROLES for part in range(PARTS)}
    free = dict.fromkeys(INBOUND, 0.0)
    waiting = {link: list(items) for link, items in INBOUND.items()}
    events = []
    while any(waiting.values()):
        ready = [
            (max(free[link], arrival[source(link, *items[0])]), link)
            for link, items in waiting.items()
            if items and source(link, *items[0]) in arrival
        ]
        start, link = min(ready)
        item = waiting[link].pop(0)
        free[link] = start + PIECE_US
        arrival[item] = start + PIECE_US + HOP_US
        issue = max(arrival[source(link, *item)], start - LEAD_US)
        events.append((issue, 0, ("send", link, item)))
    for o in range(2):
        for d in range(4):
            for group, roles in GROUPS.items():
                when = max(TOKENS_US, *(arrival[(o, d, role, part)] for role in roles for part in range(PARTS)))
                events.append((when + LATE_US, 1, ("product", (o, d), group)))
    return events


def one_hot(row, first, size):
    lines = lax.broadcasted_iota(jnp.int32, (size, row.shape[1]), 0) + first
    return (lines == row).astype(F32).astype(BF16)


def across(a, b):
    return lax.dot_general(a, b, (((1,), (1,)), ((), ())), preferred_element_type=F32)


def kernel(
    tokens, target, weight, factor_a, factor_b, counts, index, totals, asel, bsel,
    tok, tgt, buf, fb, fa, cnt, idx, acc_a, acc_w, owns, picks, brow, s_part, s_recv,
    ar_c, ar_xy, ar_z, local, send_sem, recv_sem, tok_send, tok_recv, s_send, s_got, ar_send, ar_recv,
):
    zh, x, c, zl, y = (lax.axis_index(n) for n in GRP_FSDP)
    z = zh * 2 + zl
    par = lax.rem(x, 2)
    rows, depth, cands = tokens.shape[0], weight.shape[0], counts.shape[1]
    noise = 0.5 * D ** (-0.5)

    def at(dx=0, dy=0, dz=0, dc=0):
        there = lax.rem(z + dz + 8, 8)
        return (there // 2, lax.rem(x + dx + 4, 4), lax.rem(c + dc + 2, 2), lax.rem(there, 2), lax.rem(y + dy + 4, 4))

    def piece_of(role):
        return {"m1": par, "m2": 2 + par, "t1": 1 - par, "t2": 3 - par, "c1": 4, "c2": 5}[role]

    def rows_of(d, part=0, parts=1):
        size = depth // parts
        return pl.ds(pl.multiple_of(lax.rem(y + d, 2) * 64 + part * size, 32), size)

    def columns(start, size):
        return pl.ds(pl.multiple_of(start, 128), size)

    ar_peers = [
        [dict(dc=1)],
        [dict(dx=dx, dy=dy) for dx in (2, 1, 3, 0) for dy in (2, 1, 3, 0) if dx or dy],
        [dict(dz=dz) for dz in (4, 3, 5, 2, 6, 1, 7)],
    ]
    barrier = pltpu.get_barrier_semaphore()
    near = [dict(dc=1)] + [dict(dx=i) for i in (1, 3)] + [dict(dy=i) for i in (1, 3)] + [dict(dz=i) for i in (1, 7)]
    for peer in near:
        pl.semaphore_signal(barrier, inc=1, device_id=at(**peer), device_id_type=MESH)

    copies = {}

    def bring(name, src, dst):
        copies[name] = pltpu.make_async_copy(src, dst, local.at[len(copies)])
        copies[name].start()

    for role in ROLES:
        j = piece_of(role)
        if role in ("m1", "t1"):
            src = factor_a.at[:, columns(c * 256 + j * 128, 128)]
        else:
            src = weight.at[:, columns(c * 512 + (j - 2) * 128, 128)]
        bring(role, src, buf.at[0, j, rows_of(0)])
    bring("cnt", counts, cnt)
    bring("idx", index, idx)
    bring("tok", tokens, tok.at[0])
    bring("tgt", target.at[:, columns(c * 512, 512)], tgt.at[0])
    bring("fb", factor_b, fb)
    bring("fa", factor_a, fa)

    pl.semaphore_wait(barrier, len(near))

    items = [item for link in INBOUND for item in INBOUND[link]]
    sends, waited = [], set()

    def need(item):
        if item in waited:
            return
        waited.add(item)
        o, d, role, part = item
        if (o, d) == (0, 0):
            if part == 0:
                copies[role].wait()
            return
        k = items.index(item)
        place = buf.at[o * 4 + d, piece_of(role), rows_of(d, part, PARTS)]
        pltpu.make_async_remote_copy(
            src_ref=place, dst_ref=place, send_sem=send_sem.at[k], recv_sem=recv_sem.at[k],
            device_id=at(dc=1), device_id_type=MESH,
        ).wait_recv()

    def send(link, item):
        so, sd, srole, part = source(link, *item)
        need((so, sd, srole, 0 if (so, sd) == (0, 0) else part))
        k = items.index(item)
        dx, dy, dz = LINK_STEP[link]
        j = piece_of(srole)
        copy = pltpu.make_async_remote_copy(
            src_ref=buf.at[so * 4 + sd, j, rows_of(sd, part, PARTS)],
            dst_ref=buf.at[item[0] * 4 + item[1], j, rows_of(sd, part, PARTS)],
            send_sem=send_sem.at[k], recv_sem=recv_sem.at[k],
            device_id=at(-dx, -dy, -dz), device_id_type=MESH,
        )
        copy.start()
        sends.append(copy)

    swaps = [
        pltpu.make_async_remote_copy(
            src_ref=src, dst_ref=dst, send_sem=tok_send.at[k], recv_sem=tok_recv.at[k],
            device_id=at(dc=1), device_id_type=MESH,
        )
        for k, (src, dst) in enumerate(
            ((tokens, tok.at[1]), (target.at[:, columns((1 - c) * 512, 512)], tgt.at[1]))
        )
    ]

    def start_swaps():
        for copy in swaps:
            copy.start()

    def clear():
        zero = jnp.zeros((64, 128), BF16)
        for d in range(4):
            gap = pl.multiple_of((1 - lax.rem(y + d, 2)) * depth, 64)
            for o in range(2):
                for j in range(6):
                    buf[o * 4 + d, j, pl.ds(gap, 64), :] = zero

    def owners():
        copies["cnt"].wait()
        copies["idx"].wait()
        count = cnt[...]
        upto = (
            lax.broadcasted_iota(jnp.int32, (cands, cands), 0) <= lax.broadcasted_iota(jnp.int32, (cands, cands), 1)
        ).astype(F32).astype(BF16)
        high = jnp.broadcast_to((count >> 7).astype(F32), (16, cands)).astype(BF16)
        low = jnp.broadcast_to((count & 127).astype(F32), (16, cands)).astype(BF16)
        ends = jnp.dot(high, upto, preferred_element_type=F32) * 128.0 + jnp.dot(
            low, upto, preferred_element_type=F32
        )
        ends = ends[0:1, :].astype(jnp.int32)
        starts = ends - count
        for i in range(2):
            who = lax.rem(c + i, 2)
            block = ((zh * 4 + x) * 2 + who) * 8 + zl * 4 + y
            token = lax.broadcasted_iota(jnp.int32, (rows, cands), 0) + block * rows
            owns[i] = ((starts <= token) & (token < ends)).astype(F32).astype(BF16)

    def left_picks():
        left = one_hot(idx[0:1, :], c * 256, 256)
        for i in range(2):
            picks[i] = across(owns[i], left)

    def right_rows():
        copies["fb"].wait()
        right = one_hot(idx[1:2, :], 0, fb.shape[0])
        mine = fb[:, columns(c * 512, 512)]
        for i in range(2):
            chosen = across(owns[i], right).astype(BF16)
            brow[i] = jnp.dot(chosen, mine, preferred_element_type=F32)

    def chosen_left():
        copies["fa"].wait()
        left = one_hot(idx[0:1, :], 0, fa.shape[1])
        asel[...] = jnp.dot(fa[...], left, preferred_element_type=F32).astype(BF16)

    def chosen_right():
        size = (cands, cands)
        line, lane = lax.broadcasted_iota(jnp.int32, size, 0), lax.broadcasted_iota(jnp.int32, size, 1)
        row = idx[1:2, :].astype(F32)
        column = jnp.sum(jnp.where(line == lane, row, 0.0), axis=1, keepdims=True)
        right = (column == lane.astype(F32)).astype(F32).astype(BF16)
        bsel[...] = jnp.dot(right, fb[...], preferred_element_type=F32).astype(BF16)

    seen, left_over = set(), {"a": 8}
    s_copies = [
        pltpu.make_async_remote_copy(
            src_ref=s_part.at[i], dst_ref=s_recv.at[1 - i], send_sem=s_send.at[i], recv_sem=s_got.at[i],
            device_id=at(dc=1), device_id_type=MESH,
        )
        for i in range(2)
    ]

    def product(slot, group):
        o, d = slot
        for role in GROUPS[group]:
            for part in range(PARTS):
                need((o, d, role, part))
        first = lax.rem(zl + o, 2) * 4 + lax.rem(y + d, 4)
        window = columns(first // 2 * 896 + lax.rem(first, 2) * 384, 512)
        j = "apq".index(group) * 2
        block = jnp.concatenate([buf[o * 4 + d, j], buf[o * 4 + d, j + 1]], axis=1)
        acc, lanes = (acc_a, slice(0, 256)) if group == "a" else (acc_w, slice(j * 128 - 256, j * 128))
        for i in range(2):
            if i == 0 and "tok" not in waited:
                copies["tok"].wait()
            if i == 1 and "tok" not in waited:
                swaps[0].wait_recv()
                waited.add("tok")
            part = jnp.dot(tok[i, :, window], block, preferred_element_type=F32)
            if group in seen:
                acc[i, :, lanes] += part
            else:
                acc[i, :, lanes] = part
        seen.add(group)
        if group == "a":
            left_over["a"] -= 1
            if left_over["a"] == 0:
                for i in range(2):
                    kept = jnp.where(picks[i] > 0.5, acc_a[i], 0.0)
                    s_part[i] = kept[:, :128] + kept[:, 128:]
                    s_copies[i].start()

    def perturb():
        copies["tgt"].wait()
        swaps[1].wait_recv()
        for copy in s_copies:
            copy.wait_recv()
        for i in range(2):
            score = jnp.sum(s_part[i] + s_recv[i], axis=1, keepdims=True) * noise
            acc_w[i] += score * brow[i] - tgt[i].astype(F32)

    events = timeline()
    after_a = max(when for when, _, what in events if what[0] == "product" and what[2] == "a")
    events += [
        (0.05, 2, (start_swaps,)), (0.1, 2, (clear,)), (0.5, 2, (owners,)), (1.0, 2, (left_picks,)), (1.5, 2, (right_rows,)),
        (after_a + 1.2, 2, (perturb,)),
    ]
    for _, _, what in sorted(events, key=lambda event: event[:2]):
        if what[0] == "send":
            send(*what[1:])
        elif what[0] == "product":
            product(*what[1:])
        else:
            what[0]()

    total = jnp.zeros((1, cands), F32)
    for i in range(2):
        diff = acc_w[i]
        square = diff * diff
        square = (square[:, :128] + square[:, 128:256]) + (square[:, 256:384] + square[:, 384:])
        loss = jnp.sum(square, axis=1, keepdims=True) * (1.0 / 1024)
        total += jnp.sum(owns[i].astype(F32) * loss, axis=0, keepdims=True)
    first = 0
    for group, ring, me, number in (
        (ar_peers[0], ar_c, c, lambda dc: 1 - c),
        (ar_peers[1], ar_xy, x * 4 + y, lambda dx, dy: lax.rem(x - dx + 4, 4) * 4 + lax.rem(y - dy + 4, 4)),
        (ar_peers[2], ar_z, z, lambda dz: lax.rem(z - dz + 8, 8)),
    ):
        ring[me] = total
        out = [
            pltpu.make_async_remote_copy(
                src_ref=ring.at[me], dst_ref=ring.at[me], send_sem=ar_send.at[first + k], recv_sem=ar_recv.at[first + k],
                device_id=at(**peer), device_id_type=MESH,
            )
            for k, peer in enumerate(group)
        ]
        for copy in out:
            copy.start()
        if group is ar_peers[1]:
            chosen_left()
            chosen_right()
        for k, peer in enumerate(group):
            place = ring.at[number(**peer)]
            pltpu.make_async_remote_copy(
                src_ref=place, dst_ref=place, send_sem=ar_send.at[first + k], recv_sem=ar_recv.at[first + k],
                device_id=at(**peer), device_id_type=MESH,
            ).wait_recv()
        total = ring[0]
        for k in range(1, ring.shape[0]):
            total += ring[k]
        sends.extend(out)
        first += len(group)
    totals[...] = total
    for copy in sends + swaps + s_copies:
        copy.wait_send()


def gather_and_sum(tokens, target, weight, factor_a, factor_b, counts, index):
    rows, depth = tokens.shape[0], weight.shape[0]
    cands, pool, out = counts.shape[1], factor_a.shape[1], weight.shape[1]
    links = sum(map(len, INBOUND.values()))
    dma = pltpu.SemaphoreType.DMA
    return pl.pallas_call(
        kernel,
        name="gather_and_sum",
        out_shape=(
            jax.ShapeDtypeStruct((1, cands), F32),
            jax.ShapeDtypeStruct((depth, cands), BF16),
            jax.ShapeDtypeStruct((cands, out), BF16),
        ),
        in_specs=[pl.BlockSpec(memory_space=pltpu.HBM)] * 7,
        out_specs=(pl.BlockSpec(memory_space=pltpu.VMEM),) * 3,
        scratch_shapes=[
            pltpu.VMEM((2, rows, D), BF16),
            pltpu.VMEM((2, rows, out // 2), BF16),
            pltpu.VMEM((8, 6, depth + 64, 128), BF16),
            pltpu.VMEM((pool, out), BF16),
            pltpu.VMEM((depth, pool), BF16),
            pltpu.VMEM((1, cands), jnp.int32),
            pltpu.VMEM((2, cands), jnp.int32),
            pltpu.VMEM((2, rows, pool // 2), F32),
            pltpu.VMEM((2, rows, out // 2), F32),
            pltpu.VMEM((2, rows, cands), BF16),
            pltpu.VMEM((2, rows, pool // 2), F32),
            pltpu.VMEM((2, rows, out // 2), F32),
            pltpu.VMEM((2, rows, 128), F32),
            pltpu.VMEM((2, rows, 128), F32),
            pltpu.VMEM((2, 1, cands), F32),
            pltpu.VMEM((16, 1, cands), F32),
            pltpu.VMEM((8, 1, cands), F32),
            dma((12,)),
            dma((links,)),
            dma((links,)),
            dma((2,)),
            dma((2,)),
            dma((2,)),
            dma((2,)),
            dma((23,)),
            dma((23,)),
        ],
        compiler_params=pltpu.CompilerParams(collective_id=0, has_side_effects=True, vmem_limit_bytes=40 << 20),
    )(*(pltpu.with_memory_space_constraint(a, pltpu.HBM) for a in (tokens, target, weight, factor_a, factor_b, counts, index)))


def finish_kernel(totals, counts, asel, bsel, update, scores, block, sem):
    cands, steps = counts.shape[1], block.shape[0]
    size = block.shape[1]
    fitness = -totals[...] / counts[...].astype(F32)
    middle = jnp.mean(fitness, axis=1, keepdims=True)
    spread = jnp.mean((fitness - middle) ** 2, axis=1, keepdims=True)
    score = (fitness - middle) / jnp.sqrt(spread + 1e-06)
    scores[...] = score
    out = []
    for k in range(steps):
        lines = slice(k * size, (k + 1) * size)
        scaled = (asel[lines, :].astype(F32) * score).astype(BF16)
        block[k] = jnp.dot(scaled, bsel[...], preferred_element_type=F32) * (cands**-0.5)
        copy = pltpu.make_async_copy(block.at[k], update.at[lines, :], sem.at[k])
        copy.start()
        out.append(copy)
    for copy in out:
        copy.wait()


def finish(totals, counts, asel, bsel):
    depth, cands = asel.shape
    out = bsel.shape[1]
    steps = 4
    vmem = pl.BlockSpec(memory_space=pltpu.VMEM)
    return pl.pallas_call(
        finish_kernel,
        name="finish",
        out_shape=(jax.ShapeDtypeStruct((depth, out), F32), jax.ShapeDtypeStruct((1, cands), F32)),
        in_specs=[vmem] * 4,
        out_specs=(pl.BlockSpec(memory_space=pltpu.HBM), vmem),
        scratch_shapes=[pltpu.VMEM((steps, depth // steps, out), F32), pltpu.SemaphoreType.DMA((steps,))],
        compiler_params=pltpu.CompilerParams(vmem_limit_bytes=16 << 20),
    )(totals, counts, asel, bsel)


def per_device(tokens, target, weight, factor_a, factor_b, counts, cand_index):
    counts = counts.reshape(1, -1)
    totals, asel, bsel = gather_and_sum(tokens, target, weight, factor_a, factor_b, counts, cand_index.T)
    update, scores = finish(totals, counts, asel, bsel)
    return (update, scores.reshape(-1))


def solution(mesh):
    split = Mesh(mesh.devices.reshape(4, 4, 2, 2, 4), GRP_FSDP)
    placed = (P(GRP_FSDP, None), P(GRP_FSDP, None), P(FSDP, None), P(FSDP, None), P(), P(), P())
    return jax.shard_map(
        per_device, mesh=split, in_specs=placed, out_specs=(P(FSDP, None), P()), check_vma=False
    )
```

```python
import functools

import jax
import jax.numpy as jnp
from jax import lax
from jax.experimental import pallas as pl
from jax.experimental.pallas import tpu as pltpu
from jax.sharding import Mesh
from jax.sharding import PartitionSpec as P

D = 3584
F32 = jnp.float32
BF16 = jnp.bfloat16
MESH = pl.DeviceIdType.MESH
FSDP = ("fsdp_0", "fsdp_1")
GRP_FSDP = ("grp_0", "grp_1", "grp_2", "fsdp_0", "fsdp_1")

INBOUND = {
    "y+": (
        (0, 1, "m1", 0), (0, 1, "m1", 1), (0, 1, "m2", 0), (0, 1, "m2", 1), (0, 2, "m1", 1), (0, 2, "m1", 0),
        (0, 2, "m2", 0), (0, 1, "c2", 1), (0, 1, "c1", 1), (0, 1, "c1", 0), (0, 1, "c2", 0), (1, 1, "c1", 1),
        (1, 1, "c2", 1), (0, 2, "c2", 1), (1, 2, "c1", 1),
    ),
    "y-": (
        (0, 3, "m1", 0), (0, 3, "m1", 1), (0, 3, "m2", 1), (0, 3, "m2", 0), (1, 3, "m1", 1), (0, 2, "m2", 1),
        (0, 3, "c2", 1), (0, 3, "c2", 0), (0, 3, "c1", 0), (0, 3, "c1", 1), (0, 2, "c2", 0), (0, 2, "c1", 0),
        (1, 3, "c1", 1), (0, 2, "c1", 1), (1, 2, "c2", 1),
    ),
    "z+": (
        (1, 0, "m1", 0), (1, 0, "m2", 0), (1, 0, "t1", 0), (1, 1, "m1", 0), (1, 1, "m1", 1), (1, 0, "c2", 0),
        (1, 0, "c1", 0), (1, 1, "m2", 0), (1, 3, "m2", 0), (1, 2, "m1", 0), (1, 2, "m2", 0), (1, 2, "m2", 1),
        (1, 3, "c2", 0), (1, 1, "c2", 0), (1, 2, "c2", 0),
    ),
    "z-": (
        (1, 0, "m1", 1), (1, 0, "m2", 1), (1, 0, "t1", 1), (1, 3, "m1", 0), (1, 0, "c1", 1), (1, 0, "c2", 1),
        (1, 1, "m2", 1), (1, 3, "m2", 1), (1, 0, "t2", 0), (1, 2, "m1", 1), (1, 3, "c2", 1), (1, 3, "c1", 0),
        (1, 2, "t1", 0), (1, 1, "c1", 0), (1, 2, "c1", 0),
    ),
    "x+": (
        (0, 3, "t1", 0), (0, 1, "t1", 1), (0, 1, "t2", 0), (0, 3, "t2", 1), (1, 1, "t1", 1), (0, 1, "t2", 1),
        (1, 1, "t1", 0), (0, 2, "t1", 0), (1, 1, "t2", 0), (0, 2, "t2", 1), (0, 2, "t2", 0), (1, 2, "t2", 0),
    ),
    "x-": (
        (0, 1, "t1", 0), (0, 3, "t1", 1), (1, 0, "t2", 1), (0, 3, "t2", 0), (1, 3, "t1", 0), (0, 2, "t1", 1),
        (1, 3, "t1", 1), (1, 3, "t2", 1), (1, 1, "t2", 1), (1, 3, "t2", 0), (1, 2, "t1", 1), (1, 2, "t2", 1),
    ),
}
LINK_STEP = {"y+": (0, 1, 0), "y-": (0, -1, 0), "z+": (0, 0, 1), "z-": (0, 0, -1), "x+": (1, 0, 0), "x-": (-1, 0, 0)}
SWAP = {"m1": "t1", "m2": "t2", "t1": "m1", "t2": "m2"}
ROLES = ("m1", "m2", "t1", "t2", "c1", "c2")
GROUPS = {"a": ("m1", "t1"), "p": ("m2", "t2"), "q": ("c1", "c2")}
PARTS = 2
PIECE_US, HOP_US, LEAD_US, TOKENS_US, LATE_US = 2.48 / PARTS, 1.7, 1.25, 5.0, 1.5


def source(link, o, d, role, part):
    if link == "y+":
        return (o, (d - 1) % 4, role, part)
    if link == "y-":
        return (o, (d + 1) % 4, role, part)
    if link[0] == "z":
        return (1 - o, d, role, part)
    return (o, d, SWAP[role], part)


def timeline():
    arrival = {(0, 0, role, part): 0.0 for role in ROLES for part in range(PARTS)}
    free = dict.fromkeys(INBOUND, 0.0)
    waiting = {link: list(items) for link, items in INBOUND.items()}
    events = []
    while any(waiting.values()):
        ready = [
            (max(free[link], arrival[source(link, *items[0])]), link)
            for link, items in waiting.items()
            if items and source(link, *items[0]) in arrival
        ]
        start, link = min(ready)
        item = waiting[link].pop(0)
        free[link] = start + PIECE_US
        arrival[item] = start + PIECE_US + HOP_US
        issue = max(arrival[source(link, *item)], start - LEAD_US)
        events.append((issue, 0, ("send", link, item)))
    for o in range(2):
        for d in range(4):
            for group, roles in GROUPS.items():
                when = max(TOKENS_US, *(arrival[(o, d, role, part)] for role in roles for part in range(PARTS)))
                events.append((when + LATE_US, 1, ("product", (o, d), group)))
    return events


def one_hot(row, first, size):
    lines = lax.broadcasted_iota(jnp.int32, (size, row.shape[1]), 0) + first
    return (lines == row).astype(F32).astype(BF16)


def across(a, b):
    return lax.dot_general(a, b, (((1,), (1,)), ((), ())), preferred_element_type=F32)


def kernel(
    tokens, target, weight, factor_a, factor_b, counts, index, totals, asel, bsel,
    tok, tgt, buf, fb, fa, cnt, idx, acc_a, acc_w, owns, picks, brow, s_part, s_recv,
    ar_c, ar_xy, ar_z, local, send_sem, recv_sem, tok_send, tok_recv, s_send, s_got, ar_send, ar_recv,
):
    zh, x, c, zl, y = (lax.axis_index(n) for n in GRP_FSDP)
    z = zh * 2 + zl
    par = lax.rem(x, 2)
    rows, depth, cands = tokens.shape[0], weight.shape[0], counts.shape[1]
    noise = 0.5 * D ** (-0.5)

    def at(dx=0, dy=0, dz=0, dc=0):
        there = lax.rem(z + dz + 8, 8)
        return (there // 2, lax.rem(x + dx + 4, 4), lax.rem(c + dc + 2, 2), lax.rem(there, 2), lax.rem(y + dy + 4, 4))

    def piece_of(role):
        return {"m1": par, "m2": 2 + par, "t1": 1 - par, "t2": 3 - par, "c1": 4, "c2": 5}[role]

    def rows_of(d, part=0, parts=1):
        size = depth // parts
        return pl.ds(pl.multiple_of(lax.rem(y + d, 2) * 64 + part * size, 32), size)

    def columns(start, size):
        return pl.ds(pl.multiple_of(start, 128), size)

    ar_peers = [
        [dict(dc=1)],
        [dict(dx=dx, dy=dy) for dx in (2, 1, 3, 0) for dy in (2, 1, 3, 0) if dx or dy],
        [dict(dz=dz) for dz in (4, 3, 5, 2, 6, 1, 7)],
    ]
    barrier = pltpu.get_barrier_semaphore()
    near = [dict(dc=1)] + [dict(dx=i) for i in (1, 3)] + [dict(dy=i) for i in (1, 3)] + [dict(dz=i) for i in (1, 7)]
    for peer in near:
        pl.semaphore_signal(barrier, inc=1, device_id=at(**peer), device_id_type=MESH)

    copies = {}

    def bring(name, src, dst):
        copies[name] = pltpu.make_async_copy(src, dst, local.at[len(copies)])
        copies[name].start()

    for role in ROLES:
        j = piece_of(role)
        if role in ("m1", "t1"):
            src = factor_a.at[:, columns(c * 256 + j * 128, 128)]
        else:
            src = weight.at[:, columns(c * 512 + (j - 2) * 128, 128)]
        bring(role, src, buf.at[0, j, rows_of(0)])
    bring("cnt", counts, cnt)
    bring("idx", index, idx)
    bring("tok", tokens, tok.at[0])
    bring("tgt", target.at[:, columns(c * 512, 512)], tgt.at[0])
    bring("fb", factor_b, fb)
    bring("fa", factor_a, fa)

    pl.semaphore_wait(barrier, len(near))

    items = [item for link in INBOUND for item in INBOUND[link]]
    sends, waited = [], set()

    def need(item):
        if item in waited:
            return
        waited.add(item)
        o, d, role, part = item
        if (o, d) == (0, 0):
            if part == 0:
                copies[role].wait()
            return
        k = items.index(item)
        place = buf.at[o * 4 + d, piece_of(role), rows_of(d, part, PARTS)]
        pltpu.make_async_remote_copy(
            src_ref=place, dst_ref=place, send_sem=send_sem.at[k], recv_sem=recv_sem.at[k],
            device_id=at(dc=1), device_id_type=MESH,
        ).wait_recv()

    def send(link, item):
        so, sd, srole, part = source(link, *item)
        need((so, sd, srole, 0 if (so, sd) == (0, 0) else part))
        k = items.index(item)
        dx, dy, dz = LINK_STEP[link]
        j = piece_of(srole)
        copy = pltpu.make_async_remote_copy(
            src_ref=buf.at[so * 4 + sd, j, rows_of(sd, part, PARTS)],
            dst_ref=buf.at[item[0] * 4 + item[1], j, rows_of(sd, part, PARTS)],
            send_sem=send_sem.at[k], recv_sem=recv_sem.at[k],
            device_id=at(-dx, -dy, -dz), device_id_type=MESH,
        )
        copy.start()
        sends.append(copy)

    swaps = [
        pltpu.make_async_remote_copy(
            src_ref=src, dst_ref=dst, send_sem=tok_send.at[k], recv_sem=tok_recv.at[k],
            device_id=at(dc=1), device_id_type=MESH,
        )
        for k, (src, dst) in enumerate(
            ((tokens, tok.at[1]), (target.at[:, columns((1 - c) * 512, 512)], tgt.at[1]))
        )
    ]

    def start_swaps():
        for copy in swaps:
            copy.start()

    def clear():
        zero = jnp.zeros((64, 128), BF16)
        for d in range(4):
            gap = pl.multiple_of((1 - lax.rem(y + d, 2)) * depth, 64)
            for o in range(2):
                for j in range(6):
                    buf[o * 4 + d, j, pl.ds(gap, 64), :] = zero

    def owners():
        copies["cnt"].wait()
        copies["idx"].wait()
        count = cnt[...]
        upto = (
            lax.broadcasted_iota(jnp.int32, (cands, cands), 0) <= lax.broadcasted_iota(jnp.int32, (cands, cands), 1)
        ).astype(F32).astype(BF16)
        high = jnp.broadcast_to((count >> 7).astype(F32), (16, cands)).astype(BF16)
        low = jnp.broadcast_to((count & 127).astype(F32), (16, cands)).astype(BF16)
        ends = jnp.dot(high, upto, preferred_element_type=F32) * 128.0 + jnp.dot(
            low, upto, preferred_element_type=F32
        )
        ends = ends[0:1, :].astype(jnp.int32)
        starts = ends - count
        for i in range(2):
            who = lax.rem(c + i, 2)
            block = ((zh * 4 + x) * 2 + who) * 8 + zl * 4 + y
            token = lax.broadcasted_iota(jnp.int32, (rows, cands), 0) + block * rows
            owns[i] = ((starts <= token) & (token < ends)).astype(F32).astype(BF16)

    def left_picks():
        left = one_hot(idx[0:1, :], c * 256, 256)
        for i in range(2):
            picks[i] = across(owns[i], left)

    def right_rows():
        copies["fb"].wait()
        right = one_hot(idx[1:2, :], 0, fb.shape[0])
        mine = fb[:, columns(c * 512, 512)]
        for i in range(2):
            chosen = across(owns[i], right).astype(BF16)
            brow[i] = jnp.dot(chosen, mine, preferred_element_type=F32)

    def chosen_left():
        copies["fa"].wait()
        left = one_hot(idx[0:1, :], 0, fa.shape[1])
        asel[...] = jnp.dot(fa[...], left, preferred_element_type=F32).astype(BF16)

    def chosen_right():
        size = (cands, cands)
        line, lane = lax.broadcasted_iota(jnp.int32, size, 0), lax.broadcasted_iota(jnp.int32, size, 1)
        row = idx[1:2, :].astype(F32)
        column = jnp.sum(jnp.where(line == lane, row, 0.0), axis=1, keepdims=True)
        right = (column == lane.astype(F32)).astype(F32).astype(BF16)
        bsel[...] = jnp.dot(right, fb[...], preferred_element_type=F32).astype(BF16)

    seen, left_over = set(), {"a": 8}
    s_copies = [
        pltpu.make_async_remote_copy(
            src_ref=s_part.at[i], dst_ref=s_recv.at[1 - i], send_sem=s_send.at[i], recv_sem=s_got.at[i],
            device_id=at(dc=1), device_id_type=MESH,
        )
        for i in range(2)
    ]

    def product(slot, group):
        o, d = slot
        for role in GROUPS[group]:
            for part in range(PARTS):
                need((o, d, role, part))
        first = lax.rem(zl + o, 2) * 4 + lax.rem(y + d, 4)
        window = columns(first // 2 * 896 + lax.rem(first, 2) * 384, 512)
        j = "apq".index(group) * 2
        block = jnp.concatenate([buf[o * 4 + d, j], buf[o * 4 + d, j + 1]], axis=1)
        acc, lanes = (acc_a, slice(0, 256)) if group == "a" else (acc_w, slice(j * 128 - 256, j * 128))
        for i in range(2):
            if i == 0 and "tok" not in waited:
                copies["tok"].wait()
            if i == 1 and "tok" not in waited:
                swaps[0].wait_recv()
                waited.add("tok")
            part = jnp.dot(tok[i, :, window], block, preferred_element_type=F32)
            if group in seen:
                acc[i, :, lanes] += part
            else:
                acc[i, :, lanes] = part
        seen.add(group)
        if group == "a":
            left_over["a"] -= 1
            if left_over["a"] == 0:
                for i in range(2):
                    kept = jnp.where(picks[i] > 0.5, acc_a[i], 0.0)
                    s_part[i] = kept[:, :128] + kept[:, 128:]
                    s_copies[i].start()

    def perturb():
        copies["tgt"].wait()
        swaps[1].wait_recv()
        for copy in s_copies:
            copy.wait_recv()
        for i in range(2):
            score = jnp.sum(s_part[i] + s_recv[i], axis=1, keepdims=True) * noise
            acc_w[i] += score * brow[i] - tgt[i].astype(F32)

    events = timeline()
    after_a = max(when for when, _, what in events if what[0] == "product" and what[2] == "a")
    events += [
        (0.05, 2, (start_swaps,)), (0.1, 2, (clear,)), (0.5, 2, (owners,)), (1.0, 2, (left_picks,)), (1.5, 2, (right_rows,)),
        (after_a + 1.2, 2, (perturb,)),
    ]
    for _, _, what in sorted(events, key=lambda event: event[:2]):
        if what[0] == "send":
            send(*what[1:])
        elif what[0] == "product":
            product(*what[1:])
        else:
            what[0]()

    total = jnp.zeros((1, cands), F32)
    for i in range(2):
        diff = acc_w[i]
        square = diff * diff
        square = (square[:, :128] + square[:, 128:256]) + (square[:, 256:384] + square[:, 384:])
        loss = jnp.sum(square, axis=1, keepdims=True) * (1.0 / 1024)
        total += jnp.sum(owns[i].astype(F32) * loss, axis=0, keepdims=True)
    first = 0
    for group, ring, me, number in (
        (ar_peers[0], ar_c, c, lambda dc: 1 - c),
        (ar_peers[1], ar_xy, x * 4 + y, lambda dx, dy: lax.rem(x - dx + 4, 4) * 4 + lax.rem(y - dy + 4, 4)),
        (ar_peers[2], ar_z, z, lambda dz: lax.rem(z - dz + 8, 8)),
    ):
        ring[me] = total
        out = [
            pltpu.make_async_remote_copy(
                src_ref=ring.at[me], dst_ref=ring.at[me], send_sem=ar_send.at[first + k], recv_sem=ar_recv.at[first + k],
                device_id=at(**peer), device_id_type=MESH,
            )
            for k, peer in enumerate(group)
        ]
        for copy in out:
            copy.start()
        if group is ar_peers[1]:
            chosen_left()
            chosen_right()
        for k, peer in enumerate(group):
            place = ring.at[number(**peer)]
            pltpu.make_async_remote_copy(
                src_ref=place, dst_ref=place, send_sem=ar_send.at[first + k], recv_sem=ar_recv.at[first + k],
                device_id=at(**peer), device_id_type=MESH,
            ).wait_recv()
        total = ring[0]
        for k in range(1, ring.shape[0]):
            total += ring[k]
        sends.extend(out)
        first += len(group)
    totals[...] = total
    for copy in sends + swaps + s_copies:
        copy.wait_send()


def gather_and_sum(tokens, target, weight, factor_a, factor_b, counts, index):
    rows, depth = tokens.shape[0], weight.shape[0]
    cands, pool, out = counts.shape[1], factor_a.shape[1], weight.shape[1]
    links = sum(map(len, INBOUND.values()))
    dma = pltpu.SemaphoreType.DMA
    return pl.pallas_call(
        kernel,
        name="gather_and_sum",
        out_shape=(
            jax.ShapeDtypeStruct((1, cands), F32),
            jax.ShapeDtypeStruct((depth, cands), BF16),
            jax.ShapeDtypeStruct((cands, out), BF16),
        ),
        in_specs=[pl.BlockSpec(memory_space=pltpu.HBM)] * 7,
        out_specs=(pl.BlockSpec(memory_space=pltpu.VMEM),) * 3,
        scratch_shapes=[
            pltpu.VMEM((2, rows, D), BF16),
            pltpu.VMEM((2, rows, out // 2), BF16),
            pltpu.VMEM((8, 6, depth + 64, 128), BF16),
            pltpu.VMEM((pool, out), BF16),
            pltpu.VMEM((depth, pool), BF16),
            pltpu.VMEM((1, cands), jnp.int32),
            pltpu.VMEM((2, cands), jnp.int32),
            pltpu.VMEM((2, rows, pool // 2), F32),
            pltpu.VMEM((2, rows, out // 2), F32),
            pltpu.VMEM((2, rows, cands), BF16),
            pltpu.VMEM((2, rows, pool // 2), F32),
            pltpu.VMEM((2, rows, out // 2), F32),
            pltpu.VMEM((2, rows, 128), F32),
            pltpu.VMEM((2, rows, 128), F32),
            pltpu.VMEM((2, 1, cands), F32),
            pltpu.VMEM((16, 1, cands), F32),
            pltpu.VMEM((8, 1, cands), F32),
            dma((12,)),
            dma((links,)),
            dma((links,)),
            dma((2,)),
            dma((2,)),
            dma((2,)),
            dma((2,)),
            dma((23,)),
            dma((23,)),
        ],
        compiler_params=pltpu.CompilerParams(collective_id=0, has_side_effects=True, vmem_limit_bytes=40 << 20),
    )(*(pltpu.with_memory_space_constraint(a, pltpu.HBM) for a in (tokens, target, weight, factor_a, factor_b, counts, index)))


def finish_kernel(totals, counts, asel, bsel, update, scores, block, sem):
    cands, steps = counts.shape[1], block.shape[0]
    size = block.shape[1]
    fitness = -totals[...] / counts[...].astype(F32)
    middle = jnp.mean(fitness, axis=1, keepdims=True)
    spread = jnp.mean((fitness - middle) ** 2, axis=1, keepdims=True)
    score = (fitness - middle) / jnp.sqrt(spread + 1e-06)
    scores[...] = score
    out = []
    for k in range(steps):
        lines = slice(k * size, (k + 1) * size)
        scaled = (asel[lines, :].astype(F32) * score).astype(BF16)
        block[k] = jnp.dot(scaled, bsel[...], preferred_element_type=F32) * (cands**-0.5)
        copy = pltpu.make_async_copy(block.at[k], update.at[lines, :], sem.at[k])
        copy.start()
        out.append(copy)
    for copy in out:
        copy.wait()


def finish(totals, counts, asel, bsel):
    depth, cands = asel.shape
    out = bsel.shape[1]
    steps = 7
    vmem = pl.BlockSpec(memory_space=pltpu.VMEM)
    return pl.pallas_call(
        finish_kernel,
        name="finish",
        out_shape=(jax.ShapeDtypeStruct((depth, out), F32), jax.ShapeDtypeStruct((1, cands), F32)),
        in_specs=[vmem] * 4,
        out_specs=(pl.BlockSpec(memory_space=pltpu.HBM), vmem),
        scratch_shapes=[pltpu.VMEM((steps, depth // steps, out), F32), pltpu.SemaphoreType.DMA((steps,))],
        compiler_params=pltpu.CompilerParams(vmem_limit_bytes=16 << 20),
    )(totals, counts, asel, bsel)


def per_device(tokens, target, weight, factor_a, factor_b, counts, cand_index):
    counts = counts.reshape(1, -1)
    totals, asel, bsel = gather_and_sum(tokens, target, weight, factor_a, factor_b, counts, cand_index.T)
    update, scores = finish(totals, counts, asel, bsel)
    return (update, scores.reshape(-1))


def solution(mesh):
    split = Mesh(mesh.devices.reshape(4, 4, 2, 2, 4), GRP_FSDP)
    placed = (P(GRP_FSDP, None), P(GRP_FSDP, None), P(FSDP, None), P(FSDP, None), P(), P(), P())
    return jax.shard_map(
        per_device, mesh=split, in_specs=placed, out_specs=(P(FSDP, None), P()), check_vma=False
    )
```
